128 devices in a mesh: dp: 32 (over y, z, core), section: 4 (over x).
Axes of the slice: x: 4, y: 4, z: 4, core: 2. Of those that a mesh axis runs over, the one named last changes fastest.
Arguments:
- hidden_in: bfloat16 [16384, 4096], P(('dp', 'section')), may hold values from -17 to 17
- segments: int32 [128, 128], P(('dp', 'section')), may hold values from 0 to 1, never falling along the last dimension, each value on 1 to 96 neighbouring positions
- forget_flags: int32 [128, 2], P(('dp', 'section')), may hold values 0 or 1
- block_plan: int32 [128], replicated, may hold values from 0 to 127, each once
- layer_gains: bfloat16 [4, 4096], P('section'), may hold values from 0.25 to 1.75
- kv_weights: bfloat16 [4, 4096, 1024], P('section', 'dp'), may hold values from -2 to 2
- frozen_states: bfloat16 [16384, 4096], P(('dp', 'section')), may hold values from -18 to 18
Outputs:
- hidden_out: bfloat16 [16384, 4096], P(('dp', 'section'))
- objective: float32 [], replicated
The draws below stay inside these ranges and needn't reach their ends.
Inputs may be any that keep to these rules, and one draw needn't show every extreme that they name: `segments`: in each block the segment numbers never fall; each of the 2 sequences has 1 to 96 tokens. `block_plan`: a permutation of the 128 block positions.
All inputs are finite; a program needn't handle non-finite values. No bound on the sum of `forget_flags` on one device may be relied on, other than what follows from the above.
Results may differ from the reference program's by a relative error of at most 0.02.
Values may be sent and summed in bfloat16 or wider, within the bound.
No kernel may reach another device: no remote copies, remote signals or barrier semaphores. Data moves between devices by JAX's collectives and lax.ppermute only.
A program may use at most 128 MiB of HBM per device.

```python
import math
import jax
import jax.numpy as jnp
import numpy as np
from jax import lax

QH = 32
KVH = 4
HS = 128
HD = 4096
GROUP = 8
BLK = 128
SEGS = 2
SEG_MOST = 96
SECTIONS = 4
NBLK = 128
TOKENS = 16384


def draw_hidden_in(key, part):
    normal_values = jax.random.normal(jax.random.fold_in(key, 11), (TOKENS, HD), jnp.float32)
    return jnp.clip(normal_values, -6.0, 6.0).astype(jnp.bfloat16)


def draw_kv_weights(key, part):
    normal_values = jax.random.normal(jax.random.fold_in(key, 23), (SECTIONS, HD, 2 * KVH * HS), jnp.float32)
    base_values = jnp.clip(normal_values, -6.0, 6.0) / jnp.sqrt(jnp.float32(HD))
    return base_values.astype(jnp.bfloat16)


def draw_frozen_states(key, part):
    key_base = jax.random.fold_in(jax.random.fold_in(key, 37), 0)
    row_ids = lax.broadcasted_iota(jnp.int32, (TOKENS, 1), 0)
    rising = 1.0 + 2.0 * (row_ids // BLK).astype(jnp.float32) / (NBLK - 1)
    base_values = jnp.clip(jax.random.normal(key_base, (TOKENS, HD), jnp.float32), -6.0, 6.0)
    return (base_values * rising).astype(jnp.bfloat16)


def place_ends(array, key, low, top_value):
    place = [jax.random.randint(jax.random.fold_in(key, axis), (), 0, length) for axis, length in enumerate(array.shape)]
    longest = array.shape.index(max(array.shape))
    neighbour = place[:longest] + [(place[longest] + 1) % array.shape[longest]] + place[longest + 1:]
    return array.at[tuple(place)].set(low).at[tuple(neighbour)].set(top_value)


def profile(count, total, bound, lean):
    weights = [(1 << 20) // math.isqrt(standing ** lean) + 1 for standing in range(2, count + 1)]
    surplus, holding = total - bound - (count - 1), [1] * (count - 1)
    while surplus > 0:
        candidates = [i for i in range(count - 1) if holding[i] < bound]
        mass, left = sum([weights[i] for i in candidates]), surplus
        for i in candidates:
            extra = min(bound - holding[i], max(1, left * weights[i] // mass), surplus)
            holding[i] = holding[i] + extra
            surplus = surplus - extra
    return np.array([bound] + holding)


def ragged(rng, count, total, reach, slope):
    if count == 2:
        one = jax.random.randint(rng, (), max(1, total - reach), min(reach, total - 1) + 1)
        return jnp.stack([one, total - one])
    tallies = jnp.asarray(profile(count, total, reach, slope), jnp.int32)
    twos = (count - 1) // 2
    source_of, sink = tallies[1:1 + 2 * twos:2], tallies[2:2 + 2 * twos:2]
    margin = jnp.minimum(source_of - 1, reach - sink)
    passed = jax.random.randint(jax.random.fold_in(rng, 1), (twos,), 0, 1 << 20) % (margin + 1)
    tallies = tallies.at[1:1 + 2 * twos:2].set(source_of - passed).at[2:2 + 2 * twos:2].set(sink + passed)
    return tallies[jax.random.permutation(jax.random.fold_in(rng, 2), count)]


def setup_inputs(seed: int = 0) -> dict:
    keys = jax.random.split(jax.random.key(seed), 8)
    return {
        "hidden_in": draw_hidden_in(jax.random.fold_in(keys[7], 71), 0),
        "segments": jax.vmap(lambda own: jnp.searchsorted(jnp.cumsum(ragged(own, SEGS, BLK, SEG_MOST, 2)), jnp.arange(BLK), side="right"))(jax.random.split(keys[1], NBLK)).reshape((NBLK, BLK)).astype(jnp.int32),
        "forget_flags": place_ends((jax.random.randint(keys[2], (NBLK, SEGS), 0, 2) < 1).astype(jnp.int32), jax.random.fold_in(keys[2], 1), 0, 1),
        "block_plan": jax.random.permutation(keys[3], NBLK).astype(jnp.int32),
        "layer_gains": jnp.clip(1.0 + 0.15 * jax.random.normal(keys[4], (SECTIONS, HD), jnp.float32), 0.25, 1.75).astype(jnp.bfloat16),
        "kv_weights": draw_kv_weights(jax.random.fold_in(keys[7], 71), 0),
        "frozen_states": draw_frozen_states(jax.random.fold_in(keys[7], 71), 0),
    }


forget_weight = 0.5

def attention_layer(states, segment_ids, weights, gain_row):
    widened = states.astype(jnp.float32)
    inverse_rms = lax.rsqrt(lax.optimization_barrier(jnp.mean(widened * widened, axis=-1, keepdims=True)) + 1e-05)
    normed = (widened * inverse_rms * gain_row.astype(jnp.float32)).astype(jnp.bfloat16)
    keys_values = jnp.dot(normed, weights, preferred_element_type=jnp.float32).astype(jnp.bfloat16)
    row_count = states.shape[0]
    head_width = KVH * HS
    key_heads = keys_values[:, :head_width].reshape(row_count, KVH, HS)
    value_heads = keys_values[:, head_width:].reshape(row_count, KVH, HS)
    query_heads = normed.reshape(row_count, KVH, GROUP, HS)
    scores = jnp.einsum('tkgd,skd->kgts', query_heads.astype(jnp.float32), key_heads.astype(jnp.float32)) / math.sqrt(HS)
    positions = jnp.arange(row_count, dtype=jnp.int32)
    allowed = (segment_ids[:, None] == segment_ids[None, :]) & (positions[None, :] <= positions[:, None])
    scores = jnp.where(allowed[None, None], scores, -jnp.inf)
    soft_weights = jax.nn.softmax(scores, axis=-1).astype(jnp.bfloat16)
    mixture = jnp.einsum('kgts,skd->tkgd', soft_weights.astype(jnp.float32), value_heads.astype(jnp.float32))
    return (widened + mixture.reshape(row_count, QH * HS)).astype(jnp.bfloat16)

def reference(hidden_in, segments, forget_flags, block_plan, layer_gains, kv_weights, frozen_states):
    blocks = hidden_in.reshape(NBLK, BLK, HD)

    def run_block(paired):
        states, segment_ids = paired
        for layer_index in range(SECTIONS):
            states = attention_layer(states, segment_ids, kv_weights[layer_index], layer_gains[layer_index])
        return states
    finished = lax.map(run_block, (blocks, segments))
    ordering = jnp.argsort(block_plan).astype(jnp.int32)
    hidden_out = jnp.take(finished, ordering, axis=0).reshape(TOKENS, HD)
    seg_range = jnp.arange(SEGS, dtype=jnp.int32)
    token_flags = lax.optimization_barrier(jnp.sum(jnp.where(segments[:, :, None] == seg_range[None, None, :], forget_flags[:, None, :], 0), axis=-1))
    routed_flags = jnp.take(token_flags, ordering, axis=0).reshape(TOKENS).astype(jnp.float32)
    difference = hidden_out.astype(jnp.float32) - frozen_states.astype(jnp.float32)
    distance = lax.optimization_barrier(jnp.mean(difference * difference, axis=-1))
    retain_total = jnp.sum((1.0 - routed_flags) * distance)
    forget_total = jnp.sum(routed_flags * distance)
    objective = (retain_total - forget_weight * forget_total) / TOKENS
    return (hidden_out, objective)
```

```python
import math

import jax
import jax.numpy as jnp
from jax import lax
from jax.experimental import pallas as pl
from jax.experimental.pallas import tpu as pltpu
from jax.sharding import PartitionSpec as P

QH = 32
KVH = 4
HS = 128
GROUP = 8
BLK = 128
HD = 4096
KVW = 2 * KVH * HS
PIECE_ROWS = 16
PIECE_COLS = 256
CHUNKS = 4

forget_weight = 0.5
ALL = ("dp", "section")


def layer_math(layer, boundary, gain_ref, w_buf, slot, w_wait, x_s, normed_s, acc_s, kv_s):
    gain = gain_ref[layer].astype(jnp.float32)

    def norm_rows(i, carry):
        rows = pl.ds(pl.multiple_of(i * 16, 16), 16)
        widened = x_s[rows, :].astype(jnp.float32)
        mean = jnp.sum(widened * widened, axis=-1, keepdims=True) * (1.0 / HD)
        normed_s[rows, :] = (widened * lax.rsqrt(mean + 1e-05) * gain).astype(jnp.bfloat16)
        return carry

    lax.fori_loop(0, BLK // 16, norm_rows, 0)
    depth = HD // CHUNKS
    for c in range(CHUNKS):
        w_wait(layer, c)
        part = jnp.dot(
            normed_s[:, c * depth : (c + 1) * depth],
            w_buf[slot, c * depth : (c + 1) * depth, :],
            preferred_element_type=jnp.float32,
        )
        if c == 0:
            acc_s[...] = part
        elif c < CHUNKS - 1:
            acc_s[...] += part
        else:
            kv_s[...] = (acc_s[...] + part).astype(jnp.bfloat16)
    t = lax.broadcasted_iota(jnp.int32, (BLK, BLK), 0)
    s = lax.broadcasted_iota(jnp.int32, (BLK, BLK), 1)
    allowed = (s <= t) & ((t < boundary) == (s < boundary))
    factor = math.log2(math.e) / math.sqrt(HS)

    def kv_head(j, carry):
        keys = kv_s[:, pl.ds(pl.multiple_of(j * HS, HS), HS)]
        values = kv_s[:, pl.ds(pl.multiple_of((j + KVH) * HS, HS), HS)]
        for g in range(GROUP):
            cols = pl.ds(pl.multiple_of((j * GROUP + g) * HS, HS), HS)
            scores = lax.dot_general(
                normed_s[:, cols], keys, (((1,), (1,)), ((), ())), preferred_element_type=jnp.float32
            )
            scores = jnp.where(allowed, scores, -jnp.inf)
            top = jnp.max(scores, axis=-1, keepdims=True)
            weights = jnp.exp2((scores - top) * factor)
            total = jnp.sum(weights, axis=-1, keepdims=True)
            probs = (weights * (1.0 / total)).astype(jnp.bfloat16)
            mixture = jnp.dot(probs, values, preferred_element_type=jnp.float32)
            x_s[:, cols] = (x_s[:, cols].astype(jnp.float32) + mixture).astype(jnp.bfloat16)
        return carry

    lax.fori_loop(0, KVH, kv_head, 0)


def layers_kernel(
    code_ref, pieces_ref, gain_ref, frozen_ref, w_ref, out_ref, part_ref,
    x_s, normed_s, acc_s, kv_s, w_buf, sems,
):
    depth = HD // CHUNKS

    def w_copy(layer, slot, c):
        return pltpu.make_async_copy(
            w_ref.at[layer, pl.ds(c * depth, depth)],
            w_buf.at[slot, pl.ds(c * depth, depth)],
            sems.at[slot, c],
        )

    for c in range(CHUNKS):
        w_copy(0, 0, c).start()
    across = HD // PIECE_COLS
    for p in range(pieces_ref.shape[0]):
        r, c = divmod(p, across)
        x_s[r * PIECE_ROWS : (r + 1) * PIECE_ROWS, c * PIECE_COLS : (c + 1) * PIECE_COLS] = pieces_ref[p]
    code = code_ref[0]
    boundary = code // 4
    for layer in range(4):
        if layer < 3:
            for c in range(CHUNKS):
                w_copy(layer + 1, (layer + 1) % 2, c).start()
        layer_math(
            layer, boundary, gain_ref, w_buf, layer % 2,
            lambda l, c: w_copy(l, l % 2, c).wait(),
            x_s, normed_s, acc_s, kv_s,
        )
    out_ref[...] = x_s[...]
    flag_first = (code // 2) % 2
    flag_second = code % 2

    def rows_distance(i, total):
        rows = pl.ds(pl.multiple_of(i * 16, 16), 16)
        gap = x_s[rows, :].astype(jnp.float32) - frozen_ref[rows, :].astype(jnp.float32)
        distance = jnp.sum(gap * gap, axis=-1, keepdims=True) * (1.0 / HD)
        t = lax.broadcasted_iota(jnp.int32, (16, 1), 0) + i * 16
        flag = jnp.where(t < boundary, flag_first, flag_second).astype(jnp.float32)
        return total + jnp.sum(((1.0 - flag) - forget_weight * flag) * distance, axis=0, keepdims=True)

    total = lax.fori_loop(0, BLK // 16, rows_distance, jnp.zeros((1, 1), jnp.float32))
    part_ref[...] = jnp.broadcast_to(total, part_ref.shape)


def run_layers(code, pieces, gains, frozen, weights):
    vmem = pl.BlockSpec(memory_space=pltpu.VMEM)
    return pl.pallas_call(
        layers_kernel,
        out_shape=(
            jax.ShapeDtypeStruct((BLK, HD), jnp.bfloat16),
            jax.ShapeDtypeStruct((8, 128), jnp.float32),
        ),
        in_specs=[
            pl.BlockSpec(memory_space=pltpu.SMEM), vmem, vmem, vmem,
            pl.BlockSpec(memory_space=pl.ANY),
        ],
        out_specs=(vmem, vmem),
        scratch_shapes=[
            pltpu.VMEM((BLK, HD), jnp.bfloat16),
            pltpu.VMEM((BLK, HD), jnp.bfloat16),
            pltpu.VMEM((BLK, KVW), jnp.float32),
            pltpu.VMEM((BLK, KVW), jnp.bfloat16),
            pltpu.VMEM((2, HD, KVW), jnp.bfloat16),
            pltpu.SemaphoreType.DMA((2, CHUNKS)),
        ],
        compiler_params=pltpu.CompilerParams(vmem_limit_bytes=40 << 20),
        name="layers",
    )(code, pieces, gains, frozen, weights)


def to_all(value):
    count = lax.axis_size("dp") * lax.axis_size("section")
    spread = jnp.broadcast_to(value.reshape(1, 1, 1), (count, 1, 1))
    return lax.all_to_all(spread, ALL, split_axis=0, concat_axis=0, tiled=True).reshape(count)


def order_kernel(plan_ref, landed_ref, ordered_ref):
    def place(b, carry):
        ordered_ref[plan_ref[b]] = landed_ref[b]
        return carry

    lax.fori_loop(0, landed_ref.shape[0], place, 0, unroll=8)


def route(hidden_in, block_plan):
    across = HD // PIECE_COLS
    pieces = (
        hidden_in.reshape(BLK // PIECE_ROWS, PIECE_ROWS, across, PIECE_COLS)
        .transpose(0, 2, 1, 3)
        .reshape(-1, PIECE_ROWS, PIECE_COLS)
    )
    landed = lax.all_to_all(pieces, ALL, split_axis=0, concat_axis=0, tiled=True)
    vmem = pl.BlockSpec(memory_space=pltpu.VMEM)
    ordered = pl.pallas_call(
        order_kernel,
        out_shape=jax.ShapeDtypeStruct(landed.shape, landed.dtype),
        in_specs=[pl.BlockSpec(memory_space=pltpu.SMEM), vmem],
        out_specs=vmem,
        name="order",
    )(block_plan, landed)
    return lax.all_to_all(ordered, ALL, split_axis=0, concat_axis=0, tiled=True)


def local(hidden_in, segments, forget_flags, block_plan, layer_gains, kv_weights, frozen_states):
    device_count = lax.axis_size("dp") * lax.axis_size("section")
    here = lax.axis_index(ALL)
    weights = lax.all_gather(kv_weights[0], ("section", "dp"), axis=0, tiled=True)
    weights = weights.reshape(4, HD, KVW)
    boundary = BLK - jnp.sum(segments[0])
    code = boundary * 4 + forget_flags[0, 0] * 2 + forget_flags[0, 1]
    codes = to_all(code)
    routed_code = jnp.sum(jnp.where(block_plan == here, codes, 0)).reshape(1)
    gains = lax.all_to_all(
        jnp.broadcast_to(layer_gains[None], (4, 1, HD)), "section", split_axis=0, concat_axis=0, tiled=True
    )
    pieces = route(hidden_in, block_plan)
    finished, part = run_layers(routed_code, pieces, gains, frozen_states, weights)
    objective = jnp.sum(to_all(part[0, 0])) / (BLK * device_count)
    return finished, objective


def solution(mesh):
    in_specs = (
        P(ALL, None),
        P(ALL, None),
        P(ALL, None),
        P(),
        P("section", None),
        P("section", "dp", None),
        P(ALL, None),
    )
    out_specs = (P(ALL, None), P())
    return jax.shard_map(local, mesh=mesh, in_specs=in_specs, out_specs=out_specs, check_vma=False)
```

```python
import math

import jax
import jax.numpy as jnp
from jax import lax
from jax.experimental import pallas as pl
from jax.experimental.pallas import tpu as pltpu
from jax.sharding import PartitionSpec as P

QH = 32
KVH = 4
HS = 128
GROUP = 8
BLK = 128
HD = 4096
KVW = 2 * KVH * HS
PIECE_ROWS = 32
CHUNKS = 4

forget_weight = 0.5
ALL = ("dp", "section")


def attend(boundary, x_s, normed_s, kv_s):
    t = lax.broadcasted_iota(jnp.int32, (BLK, BLK), 0)
    s = lax.broadcasted_iota(jnp.int32, (BLK, BLK), 1)
    allowed = (s <= t) & ((t < boundary) == (s < boundary))
    bias = jnp.where(allowed, 0.0, -jnp.inf)[None]
    factor = math.log2(math.e) / math.sqrt(HS)
    for j in range(KVH):
        keys = kv_s[:, j * HS : (j + 1) * HS]
        values = kv_s[:, (j + KVH) * HS : (j + KVH + 1) * HS]
        heads = pl.ds(j * GROUP, GROUP)
        queries = normed_s[heads].reshape(GROUP * BLK, HS)
        scores = lax.dot_general(
            queries, keys, (((1,), (1,)), ((), ())), preferred_element_type=jnp.float32
        )
        scores = scores.reshape(GROUP, BLK, BLK) + bias
        top = jnp.max(scores, axis=-1, keepdims=True)
        weights = jnp.exp2((scores - top) * factor).astype(jnp.bfloat16).reshape(GROUP * BLK, BLK)
        widened = jnp.concatenate([values, jnp.ones((BLK, HS), jnp.bfloat16)], axis=1)
        both = jnp.dot(weights, widened, preferred_element_type=jnp.float32)
        mixture = (both[:, :HS] / both[:, HS:]).reshape(GROUP, BLK, HS)
        x_s[heads] = (x_s[heads].astype(jnp.float32) + mixture).astype(jnp.bfloat16)


def normalize(gain_ref, layer, x_s, normed_s):
    def square(h, total):
        widened = x_s[h].astype(jnp.float32)
        return total + widened * widened

    squares = lax.fori_loop(0, QH, square, jnp.zeros((BLK, HS), jnp.float32), unroll=8)
    inverse = lax.rsqrt(jnp.sum(squares, axis=-1, keepdims=True) * (1.0 / HD) + 1e-05)
    inverse = jnp.broadcast_to(inverse, (BLK, HS))

    def scale(h, carry):
        gain = gain_ref[layer, h].astype(jnp.float32)
        normed_s[h] = (x_s[h].astype(jnp.float32) * inverse * gain).astype(jnp.bfloat16)
        return carry

    lax.fori_loop(0, QH, scale, 0, unroll=8)


def finish(code, x_s, frozen_ref, out_ref, part_ref):
    gaps = jnp.zeros((BLK, HS), jnp.float32)
    for h in range(QH):
        x = x_s[h]
        out_ref[:, h * HS : (h + 1) * HS] = x
        gap = x.astype(jnp.float32) - frozen_ref[:, h * HS : (h + 1) * HS].astype(jnp.float32)
        gaps += gap * gap
    t = lax.broadcasted_iota(jnp.int32, (BLK, HS), 0)
    flag = jnp.where(t < code // 4, (code // 2) % 2, code % 2).astype(jnp.float32)
    part = jnp.sum(((1.0 - flag) - forget_weight * flag) * gaps, axis=0, keepdims=True)
    part = jnp.sum(part, axis=1, keepdims=True) * (1.0 / HD)
    part_ref[...] = jnp.broadcast_to(part, part_ref.shape)


def layers_kernel(
    code_ref, pieces_ref, gain_ref, frozen_ref, w_ref, out_ref, part_ref,
    x_s, normed_s, acc_s, kv_s, w_buf, sems,
):
    depth = HD // CHUNKS
    slabs = depth // HS

    def w_copy(layer, c):
        return pltpu.make_async_copy(
            w_ref.at[layer, pl.ds(c * depth, depth)],
            w_buf.at[layer % 2, pl.ds(c * depth, depth)],
            sems.at[layer % 2, c],
        )

    for c in range(CHUNKS):
        w_copy(0, c).start()
    x_s[...] = pieces_ref[...]
    code = code_ref[0]
    for layer in range(4):
        if layer < 3:
            for c in range(CHUNKS):
                w_copy(layer + 1, c).start()
        normalize(gain_ref, layer, x_s, normed_s)
        for c in range(CHUNKS):
            w_copy(layer, c).wait()
            rows = jnp.concatenate([normed_s[c * slabs + i] for i in range(slabs)], axis=1)
            part = jnp.dot(
                rows, w_buf[layer % 2, c * depth : (c + 1) * depth, :], preferred_element_type=jnp.float32
            )
            if c == 0:
                acc_s[...] = part
            elif c < CHUNKS - 1:
                acc_s[...] += part
            else:
                kv_s[...] = (acc_s[...] + part).astype(jnp.bfloat16)
        attend(code // 4, x_s, normed_s, kv_s)
    finish(code, x_s, frozen_ref, out_ref, part_ref)


def run_layers(code, pieces, gains, frozen, weights):
    vmem = pl.BlockSpec(memory_space=pltpu.VMEM)
    return pl.pallas_call(
        layers_kernel,
        out_shape=(
            jax.ShapeDtypeStruct((BLK, HD), jnp.bfloat16),
            jax.ShapeDtypeStruct((8, 128), jnp.float32),
        ),
        in_specs=[
            pl.BlockSpec(memory_space=pltpu.SMEM), vmem, vmem, vmem,
            pl.BlockSpec(memory_space=pl.ANY),
        ],
        out_specs=(vmem, vmem),
        scratch_shapes=[
            pltpu.VMEM((QH, BLK, HS), jnp.bfloat16),
            pltpu.VMEM((QH, BLK, HS), jnp.bfloat16),
            pltpu.VMEM((BLK, KVW), jnp.float32),
            pltpu.VMEM((BLK, KVW), jnp.bfloat16),
            pltpu.VMEM((2, HD, KVW), jnp.bfloat16),
            pltpu.SemaphoreType.DMA((2, CHUNKS)),
        ],
        compiler_params=pltpu.CompilerParams(vmem_limit_bytes=40 << 20),
        name="layers",
    )(code, pieces, gains, frozen, weights)


def to_all(value):
    count = lax.axis_size("dp") * lax.axis_size("section")
    spread = jnp.broadcast_to(value.reshape(1, 1, 1), (count, 1, 1))
    return lax.all_to_all(spread, ALL, split_axis=0, concat_axis=0, tiled=True).reshape(count)


def order_kernel(plan_ref, landed_ref, ordered_ref):
    def place(b, carry):
        ordered_ref[plan_ref[b]] = landed_ref[b]
        return carry

    lax.fori_loop(0, landed_ref.shape[0], place, 0, unroll=8)


def route(hidden_in, block_plan):
    pieces = hidden_in.reshape(BLK, QH, HS).transpose(1, 0, 2).reshape(-1, PIECE_ROWS, HS)
    landed = lax.all_to_all(pieces, ALL, split_axis=0, concat_axis=0, tiled=True)
    vmem = pl.BlockSpec(memory_space=pltpu.VMEM)
    ordered = pl.pallas_call(
        order_kernel,
        out_shape=jax.ShapeDtypeStruct(landed.shape, landed.dtype),
        in_specs=[pl.BlockSpec(memory_space=pltpu.SMEM), vmem],
        out_specs=vmem,
        name="order",
    )(block_plan, landed)
    arrived = lax.all_to_all(ordered, ALL, split_axis=0, concat_axis=0, tiled=True)
    return arrived.reshape(QH, BLK, HS)


def local(hidden_in, segments, forget_flags, block_plan, layer_gains, kv_weights, frozen_states):
    device_count = lax.axis_size("dp") * lax.axis_size("section")
    here = lax.axis_index(ALL)
    weights = lax.all_gather(kv_weights[0], ("section", "dp"), axis=0, tiled=True)
    weights = weights.reshape(4, HD, KVW)
    boundary = BLK - jnp.sum(segments[0])
    code = boundary * 4 + forget_flags[0, 0] * 2 + forget_flags[0, 1]
    codes = to_all(code)
    routed_code = jnp.sum(jnp.where(block_plan == here, codes, 0)).reshape(1)
    gains = lax.all_to_all(
        jnp.broadcast_to(layer_gains[None], (4, 1, HD)), "section", split_axis=0, concat_axis=0, tiled=True
    ).reshape(4, QH, 1, HS)
    pieces = route(hidden_in, block_plan)
    finished, part = run_layers(routed_code, pieces, gains, frozen_states, weights)
    objective = jnp.sum(to_all(part[0, 0])) / (BLK * device_count)
    return finished, objective


def solution(mesh):
    in_specs = (
        P(ALL, None),
        P(ALL, None),
        P(ALL, None),
        P(),
        P("section", None),
        P("section", "dp", None),
        P(ALL, None),
    )
    out_specs = (P(ALL, None), P())
    return jax.shard_map(local, mesh=mesh, in_specs=in_specs, out_specs=out_specs, check_vma=False)
```

```python
import math

import jax
import jax.numpy as jnp
from jax import lax
from jax.experimental import pallas as pl
from jax.experimental.pallas import tpu as pltpu
from jax.sharding import PartitionSpec as P

QH = 32
KVH = 4
HS = 128
GROUP = 8
BLK = 128
HD = 4096
KVW = 2 * KVH * HS
PIECE_ROWS = 32
CHUNKS = 4

forget_weight = 0.5


def attend(boundary, x_s, normed_s, kv_s):
    t = lax.broadcasted_iota(jnp.int32, (BLK, BLK), 0)
    s = lax.broadcasted_iota(jnp.int32, (BLK, BLK), 1)
    allowed = (s <= t) & ((t < boundary) == (s < boundary))
    bias = jnp.where(allowed, 0.0, -jnp.inf)[None]
    factor = math.log2(math.e) / math.sqrt(HS)
    for j in range(KVH):
        keys = kv_s[:, j * HS : (j + 1) * HS]
        values = kv_s[:, (j + KVH) * HS : (j + KVH + 1) * HS]
        heads = pl.ds(j * GROUP, GROUP)
        queries = normed_s[heads].reshape(GROUP * BLK, HS)
        scores = lax.dot_general(
            queries, keys, (((1,), (1,)), ((), ())), preferred_element_type=jnp.float32
        )
        scores = scores.reshape(GROUP, BLK, BLK) + bias
        top = jnp.max(scores, axis=-1, keepdims=True)
        weights = jnp.exp2((scores - top) * factor).astype(jnp.bfloat16).reshape(GROUP * BLK, BLK)
        widened = jnp.concatenate([values, jnp.ones((BLK, HS), jnp.bfloat16)], axis=1)
        both = jnp.dot(weights, widened, preferred_element_type=jnp.float32)
        mixture = (both[:, :HS] / both[:, HS:]).reshape(GROUP, BLK, HS)
        x_s[heads] = (x_s[heads].astype(jnp.float32) + mixture).astype(jnp.bfloat16)


def normalize(gain_ref, layer, x_s, normed_s):
    def square(h, total):
        widened = x_s[h].astype(jnp.float32)
        return total + widened * widened

    squares = lax.fori_loop(0, QH, square, jnp.zeros((BLK, HS), jnp.float32), unroll=8)
    inverse = lax.rsqrt(jnp.sum(squares, axis=-1, keepdims=True) * (1.0 / HD) + 1e-05)
    inverse = jnp.broadcast_to(inverse, (BLK, HS))

    def scale(h, carry):
        gain = gain_ref[layer, h].astype(jnp.float32)
        normed_s[h] = (x_s[h].astype(jnp.float32) * inverse * gain).astype(jnp.bfloat16)
        return carry

    lax.fori_loop(0, QH, scale, 0, unroll=8)


def project(slabs, w_buf, w_wait, normed_s, acc_s, kv_s):
    for c in range(CHUNKS):
        w_wait(c)
        rows = jnp.concatenate([normed_s[slab] for slab in slabs[c]], axis=1)
        part = jnp.dot(
            rows, w_buf[c][...].reshape(HD // CHUNKS, KVW), preferred_element_type=jnp.float32
        )
        if c == 0:
            acc_s[...] = part
        elif c < CHUNKS - 1:
            acc_s[...] += part
        else:
            kv_s[...] = (acc_s[...] + part).astype(jnp.bfloat16)


def first_kernel(here_ref, pieces_ref, gain_ref, *refs):
    weights, (out_ref, info_ref, x_s, normed_s, acc_s, kv_s, w_buf, sems) = refs[:16], refs[16:]
    y, z, core, x = (here_ref[i] for i in range(4))
    half = HS * 2
    copies = []
    for layer in range(2):
        copies.append([[] for _ in range(CHUNKS)])
        for side in range(2):
            for part in range(2):
                for r in range(4):
                    source = weights[(side * 2 + part) * 4 + r]
                    for kind in range(2):
                        plane = lax.rem(x - layer - 2 * kind + 8, 4)
                        cols = pl.ds(kind * 512 + part * half, half)
                        if part == 0:
                            target = w_buf.at[layer, side, r, :, :, cols]
                        else:
                            target = w_buf.at[layer, side, :, r, :, cols]
                        at = (side * 2 + part) * 8 + r * 2 + kind
                        copy = pltpu.make_async_copy(source.at[:, plane], target, sems.at[layer, at])
                        copy.start()
                        for c in (2 * side, 2 * side + 1):
                            if part == 1 or r // 2 == c - 2 * side:
                                copies[layer][c].append(copy)
                                break
    for p in range(pieces_ref.shape[0]):
        h, g = divmod(p, BLK // PIECE_ROWS)
        x_s[h, g * PIECE_ROWS : (g + 1) * PIECE_ROWS] = pieces_ref[p, :PIECE_ROWS]
    info = pieces_ref[0, PIECE_ROWS:].astype(jnp.float32)
    info_ref[...] = info
    slabs = []
    for c in range(CHUNKS):
        side = c // 2
        owner = core if side == 0 else 1 - core
        slabs.append([
            lax.rem(y - ry + 4, 4) * 8 + lax.rem(z - rz + 4, 4) * 2 + owner
            for rz in (2 * (c % 2), 2 * (c % 2) + 1)
            for ry in range(4)
        ])
    boundary = info[0:1].astype(jnp.int32)
    for layer in range(2):
        normalize(gain_ref, lax.rem(x - layer + 4, 4), x_s, normed_s)

        def wait(c, layer=layer):
            for copy in copies[layer][c]:
                copy.wait()

        views = [w_buf.at[layer, c // 2, pl.ds(2 * (c % 2), 2)] for c in range(CHUNKS)]
        project(slabs, views, wait, normed_s, acc_s, kv_s)
        attend(boundary, x_s, normed_s, kv_s)
    out_ref[...] = x_s[...]


def second_kernel(
    here_ref, states_ref, info_ref, gain_ref, frozen_ref, w_ref, out_ref, part_ref,
    x_s, normed_s, acc_s, kv_s, w_buf, sems,
):
    depth = HD // CHUNKS
    copies = []
    for layer in range(2):
        copies.append([])
        for c in range(CHUNKS):
            pair = []
            for kind in range(2):
                copy = pltpu.make_async_copy(
                    w_ref.at[layer + 2 - 2 * kind, pl.ds(c * depth, depth)],
                    w_buf.at[layer, pl.ds(c * depth, depth), pl.ds(kind * 512, 512)],
                    sems.at[layer, c, kind],
                )
                copy.start()
                pair.append(copy)
            copies[layer].append(pair)
    x = here_ref[3]
    x_s[...] = states_ref[...]
    info = info_ref[...]
    boundary = info[0:1].astype(jnp.int32)
    slabs = [[c * 8 + i for i in range(8)] for c in range(CHUNKS)]
    for layer in range(2):
        normalize(gain_ref, lax.rem(x - layer + 2, 4), x_s, normed_s)

        def wait(c, layer=layer):
            for copy in copies[layer][c]:
                copy.wait()

        views = [w_buf.at[layer, pl.ds(c * depth, depth)] for c in range(CHUNKS)]
        project(slabs, views, wait, normed_s, acc_s, kv_s)
        attend(boundary, x_s, normed_s, kv_s)
    gaps = jnp.zeros((BLK, HS), jnp.float32)
    for h in range(QH):
        state = x_s[h]
        out_ref[:, h * HS : (h + 1) * HS] = state
        gap = state.astype(jnp.float32) - frozen_ref[:, h * HS : (h + 1) * HS].astype(jnp.float32)
        gaps += gap * gap
    t = lax.broadcasted_iota(jnp.int32, (BLK, HS), 0)
    flag = jnp.where(t < boundary, info[1:2], info[2:3])
    part = jnp.sum(((1.0 - flag) - forget_weight * flag) * gaps, axis=0, keepdims=True)
    part = jnp.sum(part, axis=1, keepdims=True) * (1.0 / HD)
    part_ref[...] = jnp.broadcast_to(part, part_ref.shape)


VMEM_SPEC = pl.BlockSpec(memory_space=pltpu.VMEM)
SMEM_SPEC = pl.BlockSpec(memory_space=pltpu.SMEM)
ANY_SPEC = pl.BlockSpec(memory_space=pl.ANY)


def layer_scratch():
    return [
        pltpu.VMEM((QH, BLK, HS), jnp.bfloat16),
        pltpu.VMEM((QH, BLK, HS), jnp.bfloat16),
        pltpu.VMEM((BLK, KVW), jnp.float32),
        pltpu.VMEM((BLK, KVW), jnp.bfloat16),
    ]


def run_first(here, pieces, gains, weights):
    return pl.pallas_call(
        first_kernel,
        out_shape=(
            jax.ShapeDtypeStruct((QH, BLK, HS), jnp.bfloat16),
            jax.ShapeDtypeStruct((8, HS), jnp.float32),
        ),
        in_specs=[SMEM_SPEC, VMEM_SPEC, VMEM_SPEC] + [ANY_SPEC] * 16,
        out_specs=(VMEM_SPEC, VMEM_SPEC),
        scratch_shapes=layer_scratch() + [
            pltpu.VMEM((2, 2, 4, 4, HS, KVW), jnp.bfloat16),
            pltpu.SemaphoreType.DMA((2, 32)),
        ],
        compiler_params=pltpu.CompilerParams(vmem_limit_bytes=40 << 20),
        name="first_layers",
    )(here, pieces, gains, *weights)


def run_second(here, states, info, gains, frozen, weights):
    return pl.pallas_call(
        second_kernel,
        out_shape=(
            jax.ShapeDtypeStruct((BLK, HD), jnp.bfloat16),
            jax.ShapeDtypeStruct((8, HS), jnp.float32),
        ),
        in_specs=[SMEM_SPEC] + [VMEM_SPEC] * 4 + [ANY_SPEC],
        out_specs=(VMEM_SPEC, VMEM_SPEC),
        scratch_shapes=layer_scratch() + [
            pltpu.VMEM((2, HD, KVW), jnp.bfloat16),
            pltpu.SemaphoreType.DMA((2, CHUNKS, 2)),
        ],
        compiler_params=pltpu.CompilerParams(vmem_limit_bytes=40 << 20),
        name="last_layers",
    )(here, states, info, gains, frozen, weights)


ALL = ("y", "z", "core", "section")


def to_all(value):
    count = lax.axis_size(ALL)
    spread = jnp.broadcast_to(value.reshape(1, 1, 1), (count, 1, 1))
    return lax.all_to_all(spread, ALL, split_axis=0, concat_axis=0, tiled=True).reshape(count)


def order_kernel(plan_ref, landed_ref, ordered_ref):
    def place(b, carry):
        ordered_ref[plan_ref[b]] = landed_ref[b]
        return carry

    lax.fori_loop(0, landed_ref.shape[0], place, 0, unroll=8)


def route(hidden_in, info, block_plan):
    pieces = hidden_in.reshape(BLK, QH, HS).transpose(1, 0, 2).reshape(-1, PIECE_ROWS, HS)
    tail = jnp.broadcast_to(info[None], (pieces.shape[0],) + info.shape)
    pieces = jnp.concatenate([pieces, tail], axis=1)
    landed = lax.all_to_all(pieces, ALL, split_axis=0, concat_axis=0, tiled=True)
    ordered = pl.pallas_call(
        order_kernel,
        out_shape=jax.ShapeDtypeStruct(landed.shape, landed.dtype),
        in_specs=[SMEM_SPEC, VMEM_SPEC],
        out_specs=VMEM_SPEC,
        name="order",
    )(block_plan, landed)
    return lax.all_to_all(ordered, ALL, split_axis=0, concat_axis=0, tiled=True)


def shifted(array, axis, by):
    peers = lax.axis_size(axis)
    return lax.ppermute(array, axis, [(i, (i + by) % peers) for i in range(peers)])


def around(array, axis):
    return [array] + [shifted(array, axis, by) for by in (1, 2, 3)]


def local(hidden_in, segments, forget_flags, block_plan, layer_gains, kv_weights, frozen_states):
    here = jnp.stack([lax.axis_index(axis) for axis in ALL]).astype(jnp.int32)
    late = here[3] >= 2
    half = KVW // 2
    keys, values = kv_weights[0, :, :half], kv_weights[0, :, half:]
    spread = shifted(values, "section", 2)
    last_weights = lax.all_gather(
        jnp.where(late, keys, spread), ("section", "y", "z", "core"), axis=0, tiled=True
    ).reshape(4, HD, half)

    boundary = BLK - jnp.sum(segments[0])
    info = jnp.concatenate([boundary.reshape(1), forget_flags[0], jnp.zeros((5,), jnp.int32)])
    info = jnp.broadcast_to(info[:, None], (8, HS)).astype(jnp.bfloat16)
    pieces = route(hidden_in, info, block_plan)

    mine = jnp.concatenate([jnp.where(late, spread, keys), layer_gains.reshape(8, half)], axis=0)
    planes = jnp.stack(around(mine, "section"))
    gains = planes[:, HS:].reshape(4, QH, 1, HS)
    left = jnp.stack(around(planes[:, :HS, : half // 2], "y"))
    right = jnp.stack(around(planes[:, :HS, half // 2 :], "z"))
    own = around(left, "z") + around(right, "y")
    other = [shifted(block, "core", 1) for block in own]
    states, info_row = run_first(here, pieces, gains, own + other)

    finished, part = run_second(here, states, info_row, gains, frozen_states, last_weights)
    objective = jnp.sum(to_all(part[0, 0])) / (BLK * lax.axis_size(ALL))
    return finished, objective


def solution(mesh):
    grid = jax.sharding.Mesh(mesh.devices.reshape(4, 4, 2, 4), ALL)
    dp = ("y", "z", "core")
    in_specs = (
        P(ALL, None),
        P(ALL, None),
        P(ALL, None),
        P(),
        P("section", None),
        P("section", dp, None),
        P(ALL, None),
    )
    out_specs = (P(ALL, None), P())
    return jax.shard_map(local, mesh=grid, in_specs=in_specs, out_specs=out_specs, check_vma=False)
```

```python
import math

import jax
import jax.numpy as jnp
from jax import lax
from jax.experimental import pallas as pl
from jax.experimental.pallas import tpu as pltpu
from jax.sharding import PartitionSpec as P

QH = 32
KVH = 4
HS = 128
GROUP = 8
BLK = 128
HD = 4096
KVW = 2 * KVH * HS
PIECE_ROWS = 32
CHUNKS = 4

forget_weight = 0.5
ALL = ("dp", "section")


def attend(boundary, x_s, normed_s, kv_s):
    t = lax.broadcasted_iota(jnp.int32, (BLK, BLK), 0)
    s = lax.broadcasted_iota(jnp.int32, (BLK, BLK), 1)
    allowed = (s <= t) & ((t < boundary) == (s < boundary))
    bias = jnp.where(allowed, 0.0, -jnp.inf)[None]
    factor = math.log2(math.e) / math.sqrt(HS)
    for j in range(KVH):
        keys = kv_s[:, j * HS : (j + 1) * HS]
        values = kv_s[:, (j + KVH) * HS : (j + KVH + 1) * HS]
        heads = pl.ds(j * GROUP, GROUP)
        queries = normed_s[heads].reshape(GROUP * BLK, HS)
        scores = lax.dot_general(
            queries, keys, (((1,), (1,)), ((), ())), preferred_element_type=jnp.float32
        )
        scores = scores.reshape(GROUP, BLK, BLK) + bias
        top = jnp.max(scores, axis=-1, keepdims=True)
        weights = jnp.exp2((scores - top) * factor).astype(jnp.bfloat16).reshape(GROUP * BLK, BLK)
        widened = jnp.concatenate([values, jnp.ones((BLK, HS), jnp.bfloat16)], axis=1)
        both = jnp.dot(weights, widened, preferred_element_type=jnp.float32)
        mixture = (both[:, :HS] / both[:, HS:]).reshape(GROUP, BLK, HS)
        x_s[heads] = (x_s[heads].astype(jnp.float32) + mixture).astype(jnp.bfloat16)


def normalize(gain_ref, layer, x_s, normed_s):
    def square(h, total):
        widened = x_s[h].astype(jnp.float32)
        return total + widened * widened

    squares = lax.fori_loop(0, QH, square, jnp.zeros((BLK, HS), jnp.float32), unroll=8)
    inverse = lax.rsqrt(jnp.sum(squares, axis=-1, keepdims=True) * (1.0 / HD) + 1e-05)
    inverse = jnp.broadcast_to(inverse, (BLK, HS))

    def scale(h, carry):
        gain = gain_ref[layer, h].astype(jnp.float32)
        normed_s[h] = (x_s[h].astype(jnp.float32) * inverse * gain).astype(jnp.bfloat16)
        return carry

    lax.fori_loop(0, QH, scale, 0, unroll=8)


def finish(code, x_s, frozen_ref, out_ref, part_ref):
    gaps = jnp.zeros((BLK, HS), jnp.float32)
    for h in range(QH):
        x = x_s[h]
        out_ref[:, h * HS : (h + 1) * HS] = x
        gap = x.astype(jnp.float32) - frozen_ref[:, h * HS : (h + 1) * HS].astype(jnp.float32)
        gaps += gap * gap
    t = lax.broadcasted_iota(jnp.int32, (BLK, HS), 0)
    flag = jnp.where(t < code // 4, (code // 2) % 2, code % 2).astype(jnp.float32)
    part = jnp.sum(((1.0 - flag) - forget_weight * flag) * gaps, axis=0, keepdims=True)
    part = jnp.sum(part, axis=1, keepdims=True) * (1.0 / HD)
    part_ref[...] = jnp.broadcast_to(part, part_ref.shape)


def layers_kernel(
    code_ref, pieces_ref, gain_ref, frozen_ref, w_ref, out_ref, part_ref,
    x_s, normed_s, acc_s, kv_s, w_buf, sems, frozen_s, frozen_sem,
):
    depth = HD // CHUNKS
    slabs = depth // HS

    def w_copy(layer, c):
        return pltpu.make_async_copy(
            w_ref.at[layer, pl.ds(c * depth, depth)],
            w_buf.at[layer % 2, pl.ds(c * depth, depth)],
            sems.at[layer % 2, c],
        )

    for c in range(CHUNKS):
        w_copy(0, c).start()
    frozen_copy = pltpu.make_async_copy(frozen_ref, frozen_s, frozen_sem)
    frozen_copy.start()
    x_s[...] = pieces_ref[...]
    code = code_ref[0]
    for layer in range(4):
        if layer < 3:
            for c in range(CHUNKS):
                w_copy(layer + 1, c).start()
        normalize(gain_ref, layer, x_s, normed_s)
        for c in range(CHUNKS):
            w_copy(layer, c).wait()
            rows = jnp.concatenate([normed_s[c * slabs + i] for i in range(slabs)], axis=1)
            part = jnp.dot(
                rows, w_buf[layer % 2, c * depth : (c + 1) * depth, :], preferred_element_type=jnp.float32
            )
            if c == 0:
                acc_s[...] = part
            elif c < CHUNKS - 1:
                acc_s[...] += part
            else:
                kv_s[...] = (acc_s[...] + part).astype(jnp.bfloat16)
        attend(code // 4, x_s, normed_s, kv_s)
    frozen_copy.wait()
    finish(code, x_s, frozen_s, out_ref, part_ref)


def run_layers(code, pieces, gains, frozen, weights):
    vmem = pl.BlockSpec(memory_space=pltpu.VMEM)
    return pl.pallas_call(
        layers_kernel,
        out_shape=(
            jax.ShapeDtypeStruct((BLK, HD), jnp.bfloat16),
            jax.ShapeDtypeStruct((128, 1, HS), jnp.float32),
        ),
        in_specs=[
            pl.BlockSpec(memory_space=pltpu.SMEM), vmem, vmem,
            pl.BlockSpec(memory_space=pl.ANY),
            pl.BlockSpec(memory_space=pl.ANY),
        ],
        out_specs=(vmem, vmem),
        scratch_shapes=[
            pltpu.VMEM((QH, BLK, HS), jnp.bfloat16),
            pltpu.VMEM((QH, BLK, HS), jnp.bfloat16),
            pltpu.VMEM((BLK, KVW), jnp.float32),
            pltpu.VMEM((BLK, KVW), jnp.bfloat16),
            pltpu.VMEM((2, HD, KVW), jnp.bfloat16),
            pltpu.SemaphoreType.DMA((2, CHUNKS)),
            pltpu.VMEM((BLK, HD), jnp.bfloat16),
            pltpu.SemaphoreType.DMA,
        ],
        compiler_params=pltpu.CompilerParams(vmem_limit_bytes=40 << 20),
        name="layers",
    )(code, pieces, gains, frozen, weights)


def to_all(value):
    count = lax.axis_size("dp") * lax.axis_size("section")
    spread = jnp.broadcast_to(value.reshape(1, 1, 1), (count, 1, 1))
    return lax.all_to_all(spread, ALL, split_axis=0, concat_axis=0, tiled=True).reshape(count)


def order_kernel(plan_ref, landed_ref, ordered_ref):
    def place(b, carry):
        ordered_ref[plan_ref[b]] = landed_ref[b]
        return carry

    lax.fori_loop(0, landed_ref.shape[0], place, 0, unroll=8)


def route(hidden_in, block_plan):
    pieces = hidden_in.reshape(BLK, QH, HS).transpose(1, 0, 2).reshape(-1, PIECE_ROWS, HS)
    landed = lax.all_to_all(pieces, ALL, split_axis=0, concat_axis=0, tiled=True)
    vmem = pl.BlockSpec(memory_space=pltpu.VMEM)
    ordered = pl.pallas_call(
        order_kernel,
        out_shape=jax.ShapeDtypeStruct(landed.shape, landed.dtype),
        in_specs=[pl.BlockSpec(memory_space=pltpu.SMEM), vmem],
        out_specs=vmem,
        name="order",
    )(block_plan, landed)
    arrived = lax.all_to_all(ordered, ALL, split_axis=0, concat_axis=0, tiled=True)
    return arrived.reshape(QH, BLK, HS)


def local(hidden_in, segments, forget_flags, block_plan, layer_gains, kv_weights, frozen_states):
    device_count = lax.axis_size("dp") * lax.axis_size("section")
    here = lax.axis_index(ALL)
    weights = lax.all_gather(kv_weights[0], ("section", "dp"), axis=0, tiled=True)
    weights = weights.reshape(4, HD, KVW)
    boundary = BLK - jnp.sum(segments[0])
    pieces = route(hidden_in, block_plan)
    sample = pieces[0, 0, 0]
    later = (sample != sample).astype(jnp.int32)
    code = boundary * 4 + forget_flags[0, 0] * 2 + forget_flags[0, 1] + later
    codes = to_all(code)
    routed_code = jnp.sum(jnp.where(block_plan == here, codes, 0)).reshape(1)
    gains = lax.all_to_all(
        jnp.broadcast_to((layer_gains + later.astype(jnp.bfloat16))[None], (4, 1, HD)), "section", split_axis=0, concat_axis=0, tiled=True
    ).reshape(4, QH, 1, HS)
    finished, part = run_layers(routed_code, pieces, gains, frozen_states, weights)
    parts = lax.all_to_all(part, ALL, split_axis=0, concat_axis=0, tiled=True)
    objective = jnp.sum(parts[:, 0, 0]) / (BLK * device_count)
    return finished, objective


def solution(mesh):
    in_specs = (
        P(ALL, None),
        P(ALL, None),
        P(ALL, None),
        P(),
        P("section", None),
        P("section", "dp", None),
        P(ALL, None),
    )
    out_specs = (P(ALL, None), P())
    return jax.shard_map(local, mesh=mesh, in_specs=in_specs, out_specs=out_specs, check_vma=False)
```

```python
import math

import jax
import jax.numpy as jnp
import numpy as np
from jax import lax
from jax.experimental import pallas as pl
from jax.experimental.pallas import tpu as pltpu
from jax.sharding import PartitionSpec as P

QH = 32
KVH = 4
HS = 128
GROUP = 8
BLK = 128
HD = 4096
KVW = 2 * KVH * HS
PIECE_ROWS = 32
CHUNKS = 4

forget_weight = 0.5
ALL = ("y", "z", "core", "section")
GATHERED = 768


def attend(boundary, x_s, normed_s, kv_s):
    t = lax.broadcasted_iota(jnp.int32, (BLK, BLK), 0)
    s = lax.broadcasted_iota(jnp.int32, (BLK, BLK), 1)
    allowed = (s <= t) & ((t < boundary) == (s < boundary))
    bias = jnp.where(allowed, 0.0, -jnp.inf)[None]
    factor = math.log2(math.e) / math.sqrt(HS)
    for j in range(KVH):
        keys = kv_s[:, j * HS : (j + 1) * HS]
        values = kv_s[:, (j + KVH) * HS : (j + KVH + 1) * HS]
        heads = pl.ds(j * GROUP, GROUP)
        queries = normed_s[heads].reshape(GROUP * BLK, HS)
        scores = lax.dot_general(
            queries, keys, (((1,), (1,)), ((), ())), preferred_element_type=jnp.float32
        )
        scores = scores.reshape(GROUP, BLK, BLK) + bias
        top = jnp.max(scores, axis=-1, keepdims=True)
        weights = jnp.exp2((scores - top) * factor).astype(jnp.bfloat16).reshape(GROUP * BLK, BLK)
        widened = jnp.concatenate([values, jnp.ones((BLK, HS), jnp.bfloat16)], axis=1)
        both = jnp.dot(weights, widened, preferred_element_type=jnp.float32)
        mixture = (both[:, :HS] / both[:, HS:]).reshape(GROUP, BLK, HS)
        x_s[heads] = (x_s[heads].astype(jnp.float32) + mixture).astype(jnp.bfloat16)


def normalize(gain_ref, layer, x_s, normed_s):
    def square(h, total):
        widened = x_s[h].astype(jnp.float32)
        return total + widened * widened

    squares = lax.fori_loop(0, QH, square, jnp.zeros((BLK, HS), jnp.float32), unroll=8)
    inverse = lax.rsqrt(jnp.sum(squares, axis=-1, keepdims=True) * (1.0 / HD) + 1e-05)
    inverse = jnp.broadcast_to(inverse, (BLK, HS))

    def scale(h, carry):
        gain = gain_ref[layer, h].astype(jnp.float32)
        normed_s[h] = (x_s[h].astype(jnp.float32) * inverse * gain).astype(jnp.bfloat16)
        return carry

    lax.fori_loop(0, QH, scale, 0, unroll=8)


def finish(code, x_s, frozen_ref, out_ref, part_ref):
    gaps = jnp.zeros((BLK, HS), jnp.float32)
    for h in range(QH):
        x = x_s[h]
        out_ref[:, h * HS : (h + 1) * HS] = x
        gap = x.astype(jnp.float32) - frozen_ref[:, h * HS : (h + 1) * HS].astype(jnp.float32)
        gaps += gap * gap
    t = lax.broadcasted_iota(jnp.int32, (BLK, HS), 0)
    flag = jnp.where(t < code // 4, (code // 2) % 2, code % 2).astype(jnp.float32)
    part = jnp.sum(((1.0 - flag) - forget_weight * flag) * gaps, axis=0, keepdims=True)
    part = jnp.sum(part, axis=1, keepdims=True) * (1.0 / HD)
    part_ref[...] = jnp.broadcast_to(part, part_ref.shape)


def layers_kernel(
    code_ref, pieces_ref, gain_ref, frozen_ref, w_ref, rest_ref, out_ref, part_ref,
    x_s, normed_s, acc_s, kv_s, w_buf, sems, frozen_s, frozen_sem,
):
    depth = HD // CHUNKS
    slabs = depth // HS

    def w_copies(layer, c):
        rows = pl.ds(c * depth, depth)
        slot = layer % 2
        return [
            pltpu.make_async_copy(
                w_ref.at[layer, rows], w_buf.at[slot, rows, pl.ds(0, GATHERED)], sems.at[slot, c, 0]
            ),
            pltpu.make_async_copy(
                rest_ref.at[layer, rows],
                w_buf.at[slot, rows, pl.ds(GATHERED, KVW - GATHERED)],
                sems.at[slot, c, 1],
            ),
        ]

    for c in range(CHUNKS):
        for copy in w_copies(0, c):
            copy.start()
    frozen_copy = pltpu.make_async_copy(frozen_ref, frozen_s, frozen_sem)
    frozen_copy.start()
    x_s[...] = pieces_ref[...]
    code = code_ref[0]
    for layer in range(4):
        if layer < 3:
            for c in range(CHUNKS):
                for copy in w_copies(layer + 1, c):
                    copy.start()
        normalize(gain_ref, layer, x_s, normed_s)
        for c in range(CHUNKS):
            for copy in w_copies(layer, c):
                copy.wait()
            rows = jnp.concatenate([normed_s[c * slabs + i] for i in range(slabs)], axis=1)
            part = jnp.dot(
                rows, w_buf[layer % 2, c * depth : (c + 1) * depth, :], preferred_element_type=jnp.float32
            )
            if c == 0:
                acc_s[...] = part
            elif c < CHUNKS - 1:
                acc_s[...] += part
            else:
                kv_s[...] = (acc_s[...] + part).astype(jnp.bfloat16)
        attend(code // 4, x_s, normed_s, kv_s)
    frozen_copy.wait()
    finish(code, x_s, frozen_s, out_ref, part_ref)


def run_layers(code, pieces, gains, frozen, weights, rest):
    vmem = pl.BlockSpec(memory_space=pltpu.VMEM)
    return pl.pallas_call(
        layers_kernel,
        out_shape=(
            jax.ShapeDtypeStruct((BLK, HD), jnp.bfloat16),
            jax.ShapeDtypeStruct((128, 1, HS), jnp.float32),
        ),
        in_specs=[
            pl.BlockSpec(memory_space=pltpu.SMEM), vmem, vmem,
            pl.BlockSpec(memory_space=pl.ANY),
            pl.BlockSpec(memory_space=pl.ANY),
            pl.BlockSpec(memory_space=pl.ANY),
        ],
        out_specs=(vmem, vmem),
        scratch_shapes=[
            pltpu.VMEM((QH, BLK, HS), jnp.bfloat16),
            pltpu.VMEM((QH, BLK, HS), jnp.bfloat16),
            pltpu.VMEM((BLK, KVW), jnp.float32),
            pltpu.VMEM((BLK, KVW), jnp.bfloat16),
            pltpu.VMEM((2, HD, KVW), jnp.bfloat16),
            pltpu.SemaphoreType.DMA((2, CHUNKS, 2)),
            pltpu.VMEM((BLK, HD), jnp.bfloat16),
            pltpu.SemaphoreType.DMA,
        ],
        compiler_params=pltpu.CompilerParams(vmem_limit_bytes=40 << 20),
        name="layers",
    )(code, pieces, gains, frozen, weights, rest)


def to_all(value):
    count = lax.axis_size(ALL)
    spread = jnp.broadcast_to(value.reshape(1, 1, 1), (count, 1, 1))
    return lax.all_to_all(spread, ALL, split_axis=0, concat_axis=0, tiled=True).reshape(count)


def order_kernel(plan_ref, landed_ref, ordered_ref):
    def place(b, carry):
        ordered_ref[plan_ref[b]] = landed_ref[b]
        return carry

    lax.fori_loop(0, landed_ref.shape[0], place, 0, unroll=8)


def route(hidden_in, block_plan):
    pieces = hidden_in.reshape(BLK, QH, HS).transpose(1, 0, 2).reshape(-1, PIECE_ROWS, HS)
    landed = lax.all_to_all(pieces, ALL, split_axis=0, concat_axis=0, tiled=True)
    vmem = pl.BlockSpec(memory_space=pltpu.VMEM)
    ordered = pl.pallas_call(
        order_kernel,
        out_shape=jax.ShapeDtypeStruct(landed.shape, landed.dtype),
        in_specs=[pl.BlockSpec(memory_space=pltpu.SMEM), vmem],
        out_specs=vmem,
        name="order",
    )(block_plan, landed)
    arrived = lax.all_to_all(ordered, ALL, split_axis=0, concat_axis=0, tiled=True)
    return arrived.reshape(QH, BLK, HS)


def assemble_kernel(here_ref, *refs):
    blocks, (rest_ref, sems) = refs[:8], refs[8:]
    y, z, core, x = (here_ref[i] for i in range(4))

    def copies(side, third, i):
        second, plane = i // 4, i % 4
        owner = core if side == 0 else 1 - core
        back_y = jnp.where(owner == 0, second, third)
        back_z = jnp.where(owner == 0, third, second)
        slab = (lax.rem(y - back_y + 4, 4) * 4 + lax.rem(z - back_z + 4, 4)) * 2 + owner
        return pltpu.make_async_copy(
            blocks[side * 4 + third].at[second, plane],
            rest_ref.at[lax.rem(x - plane + 4, 4), pl.ds(pl.multiple_of(slab * HS, HS), HS)],
            sems.at[side * 4 + third, i],
        )

    for side in range(2):
        for third in range(4):
            lax.fori_loop(0, 16, lambda i, carry: (copies(side, third, i).start(), carry)[1], 0)
    for side in range(2):
        for third in range(4):
            lax.fori_loop(0, 16, lambda i, carry: (copies(side, third, i).wait(), carry)[1], 0)


def assemble(here, blocks):
    anywhere = pl.BlockSpec(memory_space=pl.ANY)
    return pl.pallas_call(
        assemble_kernel,
        out_shape=jax.ShapeDtypeStruct((4, HD, KVW - GATHERED), jnp.bfloat16),
        in_specs=[pl.BlockSpec(memory_space=pltpu.SMEM)] + [anywhere] * 8,
        out_specs=anywhere,
        scratch_shapes=[pltpu.SemaphoreType.DMA((8, 16))],
        name="assemble",
    )(here, *blocks)


def moved(array, axes, by):
    sizes = [lax.axis_size(axis) for axis in ALL]
    pairs = []
    for at in np.ndindex(*sizes):
        to = list(at)
        axis = axes[at[2]]
        to[axis] = (to[axis] + by) % sizes[axis]
        pairs.append((int(np.ravel_multi_index(at, sizes)), int(np.ravel_multi_index(to, sizes))))
    return lax.ppermute(array, ALL, pairs)


def around(array, axes):
    return [array] + [moved(array, axes, by) for by in (1, 2, 3)]


def local(hidden_in, segments, forget_flags, block_plan, layer_gains, kv_weights, frozen_states):
    device_count = lax.axis_size(ALL)
    here = jnp.stack([lax.axis_index(axis) for axis in ALL]).astype(jnp.int32)
    index = lax.axis_index(ALL)
    weights = lax.all_gather(
        kv_weights[0, :, :GATHERED], ("section", "y", "z", "core"), axis=0, tiled=True
    ).reshape(4, HD, GATHERED)
    planes = jnp.stack(around(kv_weights[0, :, GATHERED:], (3, 3)))
    lines = jnp.stack(around(planes, (0, 1)))
    own = around(lines, (1, 0))
    rest = assemble(here, own + [moved(block, (2, 2), 1) for block in own])
    boundary = BLK - jnp.sum(segments[0])
    pieces = route(hidden_in, block_plan)
    sample = pieces[0, 0, 0]
    later = (sample != sample).astype(jnp.int32)
    code = boundary * 4 + forget_flags[0, 0] * 2 + forget_flags[0, 1] + later
    codes = to_all(code)
    routed_code = jnp.sum(jnp.where(block_plan == index, codes, 0)).reshape(1)
    gains = lax.all_to_all(
        jnp.broadcast_to((layer_gains + later.astype(jnp.bfloat16))[None], (4, 1, HD)),
        "section", split_axis=0, concat_axis=0, tiled=True,
    ).reshape(4, QH, 1, HS)
    finished, part = run_layers(routed_code, pieces, gains, frozen_states, weights, rest)
    parts = lax.all_to_all(part, ALL, split_axis=0, concat_axis=0, tiled=True)
    objective = jnp.sum(parts[:, 0, 0]) / (BLK * device_count)
    return finished, objective


def solution(mesh):
    grid = jax.sharding.Mesh(mesh.devices.reshape(4, 4, 2, 4), ALL)
    in_specs = (
        P(ALL, None),
        P(ALL, None),
        P(ALL, None),
        P(),
        P("section", None),
        P("section", ("y", "z", "core"), None),
        P(ALL, None),
    )
    out_specs = (P(ALL, None), P())
    return jax.shard_map(local, mesh=grid, in_specs=in_specs, out_specs=out_specs, check_vma=False)
```

```python
import math

import jax
import jax.numpy as jnp
from jax import lax
from jax.experimental import pallas as pl
from jax.experimental.pallas import tpu as pltpu
from jax.sharding import PartitionSpec as P

QH = 32
KVH = 4
HS = 128
GROUP = 8
BLK = 128
HD = 4096
KVW = 2 * KVH * HS
PIECE_ROWS = 32
CHUNKS = 4

forget_weight = 0.5
ALL = ("dp", "section")


def layers_kernel(
    code_ref, pieces_ref, gain_ref, frozen_ref, w_ref, out_ref, part_ref,
    x_s, scaled_s, acc_s, kv_s, w_buf, sems, frozen_s, frozen_sem,
):
    depth = HD // CHUNKS

    def w_copy(layer, c):
        rows = pl.ds(c * depth, depth)
        return pltpu.make_async_copy(
            w_ref.at[layer, rows], w_buf.at[layer, rows], sems.at[layer, c]
        )

    def prepare(layer, j, states, squares):
        heads = pl.ds(j * GROUP, GROUP)
        widened = states.astype(jnp.float32)
        gain = gain_ref[layer, heads].astype(jnp.float32)
        scaled_s[heads] = (widened * gain).astype(jnp.bfloat16)
        return squares + jnp.sum(widened * widened, axis=0)

    def project(layer, j):
        rows = jnp.concatenate([scaled_s[j * GROUP + i] for i in range(GROUP)], axis=1)
        part = jnp.dot(
            rows, w_buf[layer, j * depth : (j + 1) * depth, :], preferred_element_type=jnp.float32
        )
        if j == 0:
            acc_s[...] = part
        else:
            acc_s[...] += part

    for layer in range(2):
        for c in range(CHUNKS):
            w_copy(layer, c).start()
    frozen_copy = pltpu.make_async_copy(frozen_ref, frozen_s, frozen_sem)
    frozen_copy.start()
    code = code_ref[0]
    boundary = code // 4
    t = lax.broadcasted_iota(jnp.int32, (BLK, BLK), 0)
    s = lax.broadcasted_iota(jnp.int32, (BLK, BLK), 1)
    allowed = (s <= t) & ((t < boundary) == (s < boundary))
    bias = jnp.where(allowed, 0.0, -jnp.inf)[None]
    factor = math.log2(math.e) / math.sqrt(HS)
    squares = jnp.zeros((BLK, HS), jnp.float32)
    for j in range(KVH):
        heads = pl.ds(j * GROUP, GROUP)
        states = pieces_ref[heads]
        x_s[heads] = states
        squares = prepare(0, j, states, squares)
    for j in range(KVH):
        w_copy(0, j).wait()
        w_copy(2, j).start()
        project(0, j)
    gaps = jnp.zeros((BLK, HS), jnp.float32)
    for layer in range(4):
        inverse = lax.rsqrt(jnp.sum(squares, axis=-1, keepdims=True) * (1.0 / HD) + 1e-05)
        kv_s[...] = (acc_s[...] * inverse).astype(jnp.bfloat16)
        scale = (inverse * factor)[None]
        squares = jnp.zeros((BLK, HS), jnp.float32)
        if layer == 3:
            frozen_copy.wait()
        for j in range(KVH):
            keys = kv_s[:, j * HS : (j + 1) * HS]
            values = kv_s[:, (j + KVH) * HS : (j + KVH + 1) * HS]
            heads = pl.ds(j * GROUP, GROUP)
            queries = scaled_s[heads].reshape(GROUP * BLK, HS)
            scores = lax.dot_general(
                queries, keys, (((1,), (1,)), ((), ())), preferred_element_type=jnp.float32
            )
            scores = scores.reshape(GROUP, BLK, BLK) + bias
            top = jnp.max(scores, axis=-1, keepdims=True)
            weights = jnp.exp2((scores - top) * scale).astype(jnp.bfloat16).reshape(GROUP * BLK, BLK)
            widened = jnp.concatenate([values, jnp.ones((BLK, HS), jnp.bfloat16)], axis=1)
            both = jnp.dot(weights, widened, preferred_element_type=jnp.float32)
            mixture = (both[:, :HS] / both[:, HS:]).reshape(GROUP, BLK, HS)
            states = (x_s[heads].astype(jnp.float32) + mixture).astype(jnp.bfloat16)
            if layer < 3:
                x_s[heads] = states
                squares = prepare(layer + 1, j, states, squares)
                w_copy(layer + 1, j).wait()
                if layer == 0:
                    w_copy(3, j).start()
                project(layer + 1, j)
            else:
                for g in range(GROUP):
                    cols = slice((j * GROUP + g) * HS, (j * GROUP + g + 1) * HS)
                    out_ref[:, cols] = states[g]
                    gap = states[g].astype(jnp.float32) - frozen_s[:, cols].astype(jnp.float32)
                    gaps += gap * gap
    flag = jnp.where(t < boundary, (code // 2) % 2, code % 2).astype(jnp.float32)
    part = jnp.sum(((1.0 - flag) - forget_weight * flag) * gaps, axis=0, keepdims=True)
    part = jnp.sum(part, axis=1, keepdims=True) * (1.0 / HD)
    part_ref[...] = jnp.broadcast_to(part, part_ref.shape)


def run_layers(code, pieces, gains, frozen, weights):
    vmem = pl.BlockSpec(memory_space=pltpu.VMEM)
    return pl.pallas_call(
        layers_kernel,
        out_shape=(
            jax.ShapeDtypeStruct((BLK, HD), jnp.bfloat16),
            jax.ShapeDtypeStruct((128, 1, HS), jnp.float32),
        ),
        in_specs=[
            pl.BlockSpec(memory_space=pltpu.SMEM), vmem, vmem,
            pl.BlockSpec(memory_space=pltpu.HBM),
            pl.BlockSpec(memory_space=pltpu.HBM),
        ],
        out_specs=(vmem, vmem),
        scratch_shapes=[
            pltpu.VMEM((QH, BLK, HS), jnp.bfloat16),
            pltpu.VMEM((QH, BLK, HS), jnp.bfloat16),
            pltpu.VMEM((BLK, KVW), jnp.float32),
            pltpu.VMEM((BLK, KVW), jnp.bfloat16),
            pltpu.VMEM((4, HD, KVW), jnp.bfloat16),
            pltpu.SemaphoreType.DMA((4, CHUNKS)),
            pltpu.VMEM((BLK, HD), jnp.bfloat16),
            pltpu.SemaphoreType.DMA,
        ],
        compiler_params=pltpu.CompilerParams(vmem_limit_bytes=52 << 20),
        name="layers",
    )(code, pieces, gains, frozen, weights)


def to_all(value):
    count = lax.axis_size("dp") * lax.axis_size("section")
    spread = jnp.broadcast_to(value.reshape(1, 1, 1), (count, 1, 1))
    return lax.all_to_all(spread, ALL, split_axis=0, concat_axis=0, tiled=True).reshape(count)


def order_kernel(plan_ref, landed_ref, ordered_ref):
    def place(b, carry):
        ordered_ref[plan_ref[b]] = landed_ref[b]
        return carry

    lax.fori_loop(0, landed_ref.shape[0], place, 0, unroll=8)


def route(hidden_in, block_plan):
    pieces = hidden_in.reshape(BLK, QH, HS).transpose(1, 0, 2).reshape(-1, PIECE_ROWS, HS)
    landed = lax.all_to_all(pieces, ALL, split_axis=0, concat_axis=0, tiled=True)
    vmem = pl.BlockSpec(memory_space=pltpu.VMEM)
    ordered = pl.pallas_call(
        order_kernel,
        out_shape=jax.ShapeDtypeStruct(landed.shape, landed.dtype),
        in_specs=[pl.BlockSpec(memory_space=pltpu.SMEM), vmem],
        out_specs=vmem,
        name="order",
    )(block_plan, landed)
    arrived = lax.all_to_all(ordered, ALL, split_axis=0, concat_axis=0, tiled=True)
    return arrived.reshape(QH, BLK, HS)


def local(hidden_in, segments, forget_flags, block_plan, layer_gains, kv_weights, frozen_states):
    device_count = lax.axis_size("dp") * lax.axis_size("section")
    here = lax.axis_index(ALL)
    weights = lax.all_gather(kv_weights[0], ("section", "dp"), axis=0, tiled=True)
    weights = weights.reshape(4, HD, KVW)
    boundary = BLK - jnp.sum(segments[0])
    pieces = route(hidden_in, block_plan)
    sample = pieces[0, 0, 0]
    later = (sample != sample).astype(jnp.int32)
    code = boundary * 4 + forget_flags[0, 0] * 2 + forget_flags[0, 1] + later
    codes = to_all(code)
    routed_code = jnp.sum(jnp.where(block_plan == here, codes, 0)).reshape(1)
    gains = lax.all_to_all(
        jnp.broadcast_to((layer_gains + later.astype(jnp.bfloat16))[None], (4, 1, HD)), "section", split_axis=0, concat_axis=0, tiled=True
    ).reshape(4, QH, 1, HS)
    finished, part = run_layers(routed_code, pieces, gains, frozen_states, weights)
    parts = lax.all_to_all(part, ALL, split_axis=0, concat_axis=0, tiled=True)
    objective = jnp.sum(parts[:, 0, 0]) / (BLK * device_count)
    return finished, objective


def solution(mesh):
    in_specs = (
        P(ALL, None),
        P(ALL, None),
        P(ALL, None),
        P(),
        P("section", None),
        P("section", "dp", None),
        P(ALL, None),
    )
    out_specs = (P(ALL, None), P())
    return jax.shard_map(local, mesh=mesh, in_specs=in_specs, out_specs=out_specs, check_vma=False)
```

```python
import math

import jax
import jax.numpy as jnp
from jax import lax
from jax.experimental import pallas as pl
from jax.experimental.pallas import tpu as pltpu
from jax.sharding import PartitionSpec as P

QH = 32
KVH = 4
HS = 128
GROUP = 8
BLK = 128
HD = 4096
KVW = 2 * KVH * HS
PIECE_ROWS = 32
CHUNKS = 4

forget_weight = 0.5
ALL = ("dp", "section")


def layers_kernel(
    code_ref, pieces_ref, gain_ref, frozen_ref, w_ref, out_ref, part_ref,
    x_s, scaled_s, acc_s, kv_s, w_buf, sems, frozen_s, frozen_sem,
):
    depth = HD // CHUNKS

    def w_copy(layer, c):
        rows = pl.ds(c * depth, depth)
        return pltpu.make_async_copy(
            w_ref.at[layer, rows], w_buf.at[layer, rows], sems.at[layer, c]
        )

    def prepare(layer, j, states, squares):
        heads = pl.ds(j * GROUP, GROUP)
        widened = states.astype(jnp.float32)
        gain = gain_ref[layer, heads].astype(jnp.float32)
        scaled_s[heads] = (widened * gain).astype(jnp.bfloat16)
        return squares + jnp.sum(widened * widened, axis=0)

    def project(layer, j):
        rows = jnp.concatenate([scaled_s[j * GROUP + i] for i in range(GROUP)], axis=1)
        part = jnp.dot(
            rows, w_buf[layer, j * depth : (j + 1) * depth, :], preferred_element_type=jnp.float32
        )
        if j == 0:
            acc_s[...] = part
        else:
            acc_s[...] += part

    for layer in range(2):
        for c in range(CHUNKS):
            w_copy(layer, c).start()
    frozen_copy = pltpu.make_async_copy(frozen_ref, frozen_s, frozen_sem)
    frozen_copy.start()
    code = code_ref[0]
    boundary = code // 4
    t = lax.broadcasted_iota(jnp.int32, (BLK, BLK), 0)
    s = lax.broadcasted_iota(jnp.int32, (BLK, BLK), 1)
    allowed = (s <= t) & ((t < boundary) == (s < boundary))
    bias = jnp.where(allowed, 0.0, -jnp.inf)[None]
    factor = math.log2(math.e) / math.sqrt(HS)
    squares = jnp.zeros((BLK, HS), jnp.float32)
    for j in range(KVH):
        heads = pl.ds(j * GROUP, GROUP)
        states = pieces_ref[heads]
        x_s[heads] = states
        squares = prepare(0, j, states, squares)
    for j in range(KVH):
        w_copy(0, j).wait()
        w_copy(2, j).start()
        project(0, j)
    gaps = jnp.zeros((BLK, HS), jnp.float32)
    for layer in range(4):
        inverse = lax.rsqrt(jnp.sum(squares, axis=-1, keepdims=True) * (1.0 / HD) + 1e-05)
        kv_s[...] = (acc_s[...] * inverse).astype(jnp.bfloat16)
        scale = (inverse * factor)[None]
        squares = jnp.zeros((BLK, HS), jnp.float32)
        if layer == 3:
            frozen_copy.wait()
        for j in range(KVH):
            keys = kv_s[:, j * HS : (j + 1) * HS]
            values = kv_s[:, (j + KVH) * HS : (j + KVH + 1) * HS]
            heads = pl.ds(j * GROUP, GROUP)
            queries = scaled_s[heads].reshape(GROUP * BLK, HS)
            scores = lax.dot_general(
                queries, keys, (((1,), (1,)), ((), ())), preferred_element_type=jnp.float32
            )
            scores = scores.reshape(GROUP, BLK, BLK) + bias
            top = jnp.max(scores, axis=-1, keepdims=True)
            weights = jnp.exp2((scores - top) * scale).astype(jnp.bfloat16).reshape(GROUP * BLK, BLK)
            widened = jnp.concatenate([values, jnp.ones((BLK, HS), jnp.bfloat16)], axis=1)
            both = jnp.dot(weights, widened, preferred_element_type=jnp.float32)
            mixture = (both[:, :HS] / both[:, HS:]).reshape(GROUP, BLK, HS)
            states = (x_s[heads].astype(jnp.float32) + mixture).astype(jnp.bfloat16)
            if layer < 3:
                x_s[heads] = states
                squares = prepare(layer + 1, j, states, squares)
                w_copy(layer + 1, j).wait()
                if layer == 0:
                    w_copy(3, j).start()
                project(layer + 1, j)
            else:
                for g in range(GROUP):
                    cols = slice((j * GROUP + g) * HS, (j * GROUP + g + 1) * HS)
                    out_ref[:, cols] = states[g]
                    gap = states[g].astype(jnp.float32) - frozen_s[:, cols].astype(jnp.float32)
                    gaps += gap * gap
    flag = jnp.where(t < boundary, (code // 2) % 2, code % 2).astype(jnp.float32)
    part = jnp.sum(((1.0 - flag) - forget_weight * flag) * gaps, axis=0, keepdims=True)
    part = jnp.sum(part, axis=1, keepdims=True) * (1.0 / HD)
    part_ref[...] = jnp.broadcast_to(part, part_ref.shape)


def run_layers(code, pieces, gains, frozen, weights):
    vmem = pl.BlockSpec(memory_space=pltpu.VMEM)
    return pl.pallas_call(
        layers_kernel,
        out_shape=(
            jax.ShapeDtypeStruct((BLK, HD), jnp.bfloat16),
            jax.ShapeDtypeStruct((128, 1, HS), jnp.float32),
        ),
        in_specs=[
            pl.BlockSpec(memory_space=pltpu.SMEM), vmem, vmem,
            pl.BlockSpec(memory_space=pltpu.HBM),
            pl.BlockSpec(memory_space=pltpu.HBM),
        ],
        out_specs=(vmem, vmem),
        scratch_shapes=[
            pltpu.VMEM((QH, BLK, HS), jnp.bfloat16),
            pltpu.VMEM((QH, BLK, HS), jnp.bfloat16),
            pltpu.VMEM((BLK, KVW), jnp.float32),
            pltpu.VMEM((BLK, KVW), jnp.bfloat16),
            pltpu.VMEM((4, HD, KVW), jnp.bfloat16),
            pltpu.SemaphoreType.DMA((4, CHUNKS)),
            pltpu.VMEM((BLK, HD), jnp.bfloat16),
            pltpu.SemaphoreType.DMA,
        ],
        compiler_params=pltpu.CompilerParams(vmem_limit_bytes=52 << 20),
        name="layers",
    )(code, pieces, gains, frozen, weights)


def order_kernel(plan_ref, landed_ref, ordered_ref):
    def place(b, carry):
        ordered_ref[plan_ref[b]] = landed_ref[b]
        return carry

    lax.fori_loop(0, landed_ref.shape[0], place, 0, unroll=8)


def route(hidden_in, block_plan):
    pieces = hidden_in.reshape(BLK, QH, HS).transpose(1, 0, 2).reshape(-1, PIECE_ROWS, HS)
    landed = lax.all_to_all(pieces, ALL, split_axis=0, concat_axis=0, tiled=True)
    vmem = pl.BlockSpec(memory_space=pltpu.VMEM)
    ordered = pl.pallas_call(
        order_kernel,
        out_shape=jax.ShapeDtypeStruct(landed.shape, landed.dtype),
        in_specs=[pl.BlockSpec(memory_space=pltpu.SMEM), vmem],
        out_specs=vmem,
        name="order",
    )(block_plan, landed)
    arrived = lax.all_to_all(ordered, ALL, split_axis=0, concat_axis=0, tiled=True)
    return arrived.reshape(QH, BLK, HS)


def local(hidden_in, segments, forget_flags, block_plan, layer_gains, kv_weights, frozen_states):
    device_count = lax.axis_size("dp") * lax.axis_size("section")
    here = lax.axis_index(ALL)
    weights = lax.all_gather(kv_weights[0], ("section", "dp"), axis=0, tiled=True)
    weights = weights.reshape(4, HD, KVW)
    boundary = BLK - jnp.sum(segments[0])
    pieces = route(hidden_in, block_plan)
    sample = pieces[0, 0, 0]
    later = (sample != sample).astype(jnp.int32)
    code = jnp.concatenate([(boundary + later).reshape(1), forget_flags[0]]).astype(jnp.bfloat16)
    code = jnp.zeros((1, HS), jnp.bfloat16).at[0, :3].set(code)
    own_gains = lax.dynamic_slice(layer_gains, (0, lax.axis_index("dp") * HS), (1, HS))
    message = jnp.concatenate([own_gains, code], axis=0)
    messages = lax.all_to_all(
        jnp.broadcast_to(message[None], (device_count, 2, HS)), ALL, split_axis=0, concat_axis=0, tiled=True
    )
    gains = messages[:, 0].reshape(QH, 4, HS).transpose(1, 0, 2).reshape(4, QH, 1, HS)
    codes = messages[:, 1].astype(jnp.float32)
    routed = jnp.sum(jnp.where((block_plan == here)[:, None], codes, 0.0), axis=0)
    routed_code = (routed[0] * 4.0 + routed[1] * 2.0 + routed[2]).astype(jnp.int32).reshape(1)
    finished, part = run_layers(routed_code, pieces, gains, frozen_states, weights)
    parts = lax.all_to_all(part, ALL, split_axis=0, concat_axis=0, tiled=True)
    objective = jnp.sum(parts[:, 0, 0]) / (BLK * device_count)
    return finished, objective


def solution(mesh):
    in_specs = (
        P(ALL, None),
        P(ALL, None),
        P(ALL, None),
        P(),
        P("section", None),
        P("section", "dp", None),
        P(ALL, None),
    )
    out_specs = (P(ALL, None), P())
    return jax.shard_map(local, mesh=mesh, in_specs=in_specs, out_specs=out_specs, check_vma=False)
```

```python
import math

import jax
import jax.numpy as jnp
from jax import lax
from jax.experimental import pallas as pl
from jax.experimental.pallas import tpu as pltpu
from jax.sharding import PartitionSpec as P

QH = 32
KVH = 4
HS = 128
GROUP = 8
BLK = 128
HD = 4096
KVW = 2 * KVH * HS
PIECE_ROWS = 32
CHUNKS = 4

forget_weight = 0.5
ALL = ("dp", "section")


def layers_kernel(
    code_ref, pieces_ref, gain_ref, frozen_ref, w_ref, out_ref, part_ref,
    x_s, scaled_s, acc_s, kv_s, w_buf, sems, frozen_s, frozen_sem,
):
    depth = HD // CHUNKS

    def w_copy(layer, c):
        rows = pl.ds(c * depth, depth)
        return pltpu.make_async_copy(
            w_ref.at[layer, rows], w_buf.at[layer, rows], sems.at[layer, c]
        )

    def prepare(layer, j, states, squares):
        heads = pl.ds(j * GROUP, GROUP)
        widened = states.astype(jnp.float32)
        gain = gain_ref[layer, heads].astype(jnp.float32)
        scaled_s[heads] = (widened * gain).astype(jnp.bfloat16)
        return squares + jnp.sum(widened * widened, axis=0)

    def project(layer, j):
        rows = jnp.concatenate([scaled_s[j * GROUP + i] for i in range(GROUP)], axis=1)
        part = jnp.dot(
            rows, w_buf[layer, j * depth : (j + 1) * depth, :], preferred_element_type=jnp.float32
        )
        if j == 0:
            acc_s[...] = part
        else:
            acc_s[...] += part

    for layer in range(2):
        for c in range(CHUNKS):
            w_copy(layer, c).start()
    frozen_copy = pltpu.make_async_copy(frozen_ref, frozen_s, frozen_sem)
    frozen_copy.start()
    code = code_ref[0]
    boundary = code // 4
    t = lax.broadcasted_iota(jnp.int32, (BLK, BLK), 0)
    s = lax.broadcasted_iota(jnp.int32, (BLK, BLK), 1)
    allowed = (s <= t) & ((t < boundary) == (s < boundary))
    bias = jnp.where(allowed, 0.0, -jnp.inf)[None]
    factor = math.log2(math.e) / math.sqrt(HS)
    squares = jnp.zeros((BLK, HS), jnp.float32)
    for j in range(KVH):
        heads = pl.ds(j * GROUP, GROUP)
        states = pieces_ref[heads]
        x_s[heads] = states
        squares = prepare(0, j, states, squares)
    for j in range(KVH):
        w_copy(0, j).wait()
        w_copy(2, j).start()
        project(0, j)
    gaps = jnp.zeros((BLK, HS), jnp.float32)
    for layer in range(4):
        inverse = lax.rsqrt(jnp.sum(squares, axis=-1, keepdims=True) * (1.0 / HD) + 1e-05)
        kv_s[...] = (acc_s[...] * inverse).astype(jnp.bfloat16)
        scale = (inverse * factor)[None]
        squares = jnp.zeros((BLK, HS), jnp.float32)
        if layer == 3:
            frozen_copy.wait()
        for j in range(KVH):
            keys = kv_s[:, j * HS : (j + 1) * HS]
            values = kv_s[:, (j + KVH) * HS : (j + KVH + 1) * HS]
            heads = pl.ds(j * GROUP, GROUP)
            if j % 2 == 0:
                queries = jnp.concatenate(
                    [
                        scaled_s[heads].reshape(GROUP * BLK, HS),
                        scaled_s[pl.ds((j + 1) * GROUP, GROUP)].reshape(GROUP * BLK, HS),
                    ],
                    axis=1,
                )
                next_keys = kv_s[:, (j + 1) * HS : (j + 2) * HS]
                none = jnp.zeros((BLK, HS), jnp.bfloat16)
                both_keys = jnp.concatenate(
                    [
                        jnp.concatenate([keys, none], axis=1),
                        jnp.concatenate([none, next_keys], axis=1),
                    ],
                    axis=0,
                )
                both_scores = lax.dot_general(
                    queries, both_keys, (((1,), (1,)), ((), ())), preferred_element_type=jnp.float32
                )
            scores = both_scores[:, (j % 2) * BLK : (j % 2 + 1) * BLK]
            scores = scores.reshape(GROUP, BLK, BLK) + bias
            top = jnp.max(scores, axis=-1, keepdims=True)
            weights = jnp.exp2((scores - top) * scale).astype(jnp.bfloat16).reshape(GROUP * BLK, BLK)
            widened = jnp.concatenate([values, jnp.ones((BLK, HS), jnp.bfloat16)], axis=1)
            both = jnp.dot(weights, widened, preferred_element_type=jnp.float32)
            mixture = (both[:, :HS] / both[:, HS:]).reshape(GROUP, BLK, HS)
            states = (x_s[heads].astype(jnp.float32) + mixture).astype(jnp.bfloat16)
            if layer < 3:
                x_s[heads] = states
                squares = prepare(layer + 1, j, states, squares)
                w_copy(layer + 1, j).wait()
                if layer == 0:
                    w_copy(3, j).start()
                project(layer + 1, j)
            else:
                for g in range(GROUP):
                    cols = slice((j * GROUP + g) * HS, (j * GROUP + g + 1) * HS)
                    out_ref[:, cols] = states[g]
                    gap = states[g].astype(jnp.float32) - frozen_s[:, cols].astype(jnp.float32)
                    gaps += gap * gap
    flag = jnp.where(t < boundary, (code // 2) % 2, code % 2).astype(jnp.float32)
    part = jnp.sum(((1.0 - flag) - forget_weight * flag) * gaps, axis=0, keepdims=True)
    part = jnp.sum(part, axis=1, keepdims=True) * (1.0 / HD)
    part_ref[...] = jnp.broadcast_to(part, part_ref.shape)


def run_layers(code, pieces, gains, frozen, weights):
    vmem = pl.BlockSpec(memory_space=pltpu.VMEM)
    return pl.pallas_call(
        layers_kernel,
        out_shape=(
            jax.ShapeDtypeStruct((BLK, HD), jnp.bfloat16),
            jax.ShapeDtypeStruct((128, 1, HS), jnp.float32),
        ),
        in_specs=[
            pl.BlockSpec(memory_space=pltpu.SMEM), vmem, vmem,
            pl.BlockSpec(memory_space=pltpu.HBM),
            pl.BlockSpec(memory_space=pltpu.HBM),
        ],
        out_specs=(vmem, vmem),
        scratch_shapes=[
            pltpu.VMEM((QH, BLK, HS), jnp.bfloat16),
            pltpu.VMEM((QH, BLK, HS), jnp.bfloat16),
            pltpu.VMEM((BLK, KVW), jnp.float32),
            pltpu.VMEM((BLK, KVW), jnp.bfloat16),
            pltpu.VMEM((4, HD, KVW), jnp.bfloat16),
            pltpu.SemaphoreType.DMA((4, CHUNKS)),
            pltpu.VMEM((BLK, HD), jnp.bfloat16),
            pltpu.SemaphoreType.DMA,
        ],
        compiler_params=pltpu.CompilerParams(vmem_limit_bytes=52 << 20),
        name="layers",
    )(code, pieces, gains, frozen, weights)


def order_kernel(plan_ref, landed_ref, ordered_ref):
    def place(b, carry):
        ordered_ref[plan_ref[b]] = landed_ref[b]
        return carry

    lax.fori_loop(0, landed_ref.shape[0], place, 0, unroll=8)


def route(hidden_in, block_plan):
    pieces = hidden_in.reshape(BLK, QH, HS).transpose(1, 0, 2).reshape(-1, PIECE_ROWS, HS)
    landed = lax.all_to_all(pieces, ALL, split_axis=0, concat_axis=0, tiled=True)
    vmem = pl.BlockSpec(memory_space=pltpu.VMEM)
    ordered = pl.pallas_call(
        order_kernel,
        out_shape=jax.ShapeDtypeStruct(landed.shape, landed.dtype),
        in_specs=[pl.BlockSpec(memory_space=pltpu.SMEM), vmem],
        out_specs=vmem,
        name="order",
    )(block_plan, landed)
    arrived = lax.all_to_all(ordered, ALL, split_axis=0, concat_axis=0, tiled=True)
    return arrived.reshape(QH, BLK, HS)


def local(hidden_in, segments, forget_flags, block_plan, layer_gains, kv_weights, frozen_states):
    device_count = lax.axis_size("dp") * lax.axis_size("section")
    here = lax.axis_index(ALL)
    weights = lax.all_gather(kv_weights[0], ("section", "dp"), axis=0, tiled=True)
    weights = weights.reshape(4, HD, KVW)
    boundary = BLK - jnp.sum(segments[0])
    pieces = route(hidden_in, block_plan)
    sample = pieces[0, 0, 0]
    later = (sample != sample).astype(jnp.int32)
    code = jnp.concatenate([(boundary + later).reshape(1), forget_flags[0]]).astype(jnp.bfloat16)
    code = jnp.zeros((1, HS), jnp.bfloat16).at[0, :3].set(code)
    own_gains = lax.dynamic_slice(layer_gains, (0, lax.axis_index("dp") * HS), (1, HS))
    message = jnp.concatenate([own_gains, code], axis=0)
    messages = lax.all_to_all(
        jnp.broadcast_to(message[None], (device_count, 2, HS)), ALL, split_axis=0, concat_axis=0, tiled=True
    )
    gains = messages[:, 0].reshape(QH, 4, HS).transpose(1, 0, 2).reshape(4, QH, 1, HS)
    codes = messages[:, 1].astype(jnp.float32)
    routed = jnp.sum(jnp.where((block_plan == here)[:, None], codes, 0.0), axis=0)
    routed_code = (routed[0] * 4.0 + routed[1] * 2.0 + routed[2]).astype(jnp.int32).reshape(1)
    finished, part = run_layers(routed_code, pieces, gains, frozen_states, weights)
    parts = lax.all_to_all(part, ALL, split_axis=0, concat_axis=0, tiled=True)
    objective = jnp.sum(parts[:, 0, 0]) / (BLK * device_count)
    return finished, objective


def solution(mesh):
    in_specs = (
        P(ALL, None),
        P(ALL, None),
        P(ALL, None),
        P(),
        P("section", None),
        P("section", "dp", None),
        P(ALL, None),
    )
    out_specs = (P(ALL, None), P())
    return jax.shard_map(local, mesh=mesh, in_specs=in_specs, out_specs=out_specs, check_vma=False)
```

```python
import math

import jax
import jax.numpy as jnp
from jax import lax
from jax.experimental import pallas as pl
from jax.experimental.pallas import tpu as pltpu
from jax.sharding import PartitionSpec as P

QH = 32
KVH = 4
HS = 128
GROUP = 8
BLK = 128
HD = 4096
KVW = 2 * KVH * HS
PIECE_ROWS = 32
CHUNKS = 4

forget_weight = 0.5
ALL = ("dp", "section")


def layers_kernel(
    code_ref, pieces_ref, gain_ref, frozen_ref, w_ref, out_ref, part_ref,
    x_s, scaled_s, acc_s, kv_s, w_buf, sems, frozen_s, frozen_sem,
):
    depth = HD // CHUNKS

    def w_copy(layer, c):
        rows = pl.ds(c * depth, depth)
        return pltpu.make_async_copy(
            w_ref.at[layer, rows], w_buf.at[layer, rows], sems.at[layer, c]
        )

    def prepare(layer, j, states, squares):
        heads = pl.ds(j * GROUP, GROUP)
        widened = states.astype(jnp.float32)
        gain = gain_ref[layer, heads].astype(jnp.float32)
        scaled_s[heads] = (widened * gain).astype(jnp.bfloat16)
        return squares + jnp.sum(widened * widened, axis=0)

    def project(layer, j):
        rows = jnp.concatenate([scaled_s[j * GROUP + i] for i in range(GROUP)], axis=1)
        part = jnp.dot(
            rows, w_buf[layer, j * depth : (j + 1) * depth, :], preferred_element_type=jnp.float32
        )
        if j == 0:
            acc_s[...] = part
        else:
            acc_s[...] += part

    for layer in range(2):
        for c in range(CHUNKS):
            w_copy(layer, c).start()
    frozen_copy = pltpu.make_async_copy(frozen_ref, frozen_s, frozen_sem)
    frozen_copy.start()
    code = code_ref[0]
    boundary = code // 4
    t = lax.broadcasted_iota(jnp.int32, (BLK, BLK), 0)
    s = lax.broadcasted_iota(jnp.int32, (BLK, BLK), 1)
    allowed = (s <= t) & ((t < boundary) == (s < boundary))
    bias = jnp.where(allowed, 0.0, -jnp.inf)[None]
    factor = math.log2(math.e) / math.sqrt(HS)
    squares = jnp.zeros((BLK, HS), jnp.float32)
    for j in range(KVH):
        heads = pl.ds(j * GROUP, GROUP)
        states = pieces_ref[heads]
        x_s[heads] = states
        squares = prepare(0, j, states, squares)
    for j in range(KVH):
        w_copy(0, j).wait()
        w_copy(2, j).start()
        project(0, j)
    gaps = jnp.zeros((BLK, HS), jnp.float32)
    for layer in range(4):
        inverse = lax.rsqrt(jnp.sum(squares, axis=-1, keepdims=True) * (1.0 / HD) + 1e-05)
        kv_s[...] = (acc_s[...] * inverse).astype(jnp.bfloat16)
        scale = (inverse * factor)[None]
        squares = jnp.zeros((BLK, HS), jnp.float32)
        if layer == 3:
            frozen_copy.wait()
        for j in range(KVH):
            keys = kv_s[:, j * HS : (j + 1) * HS]
            values = kv_s[:, (j + KVH) * HS : (j + KVH + 1) * HS]
            heads = pl.ds(j * GROUP, GROUP)
            if j % 2 == 0:
                queries = jnp.concatenate(
                    [
                        scaled_s[heads].reshape(GROUP * BLK, HS),
                        scaled_s[pl.ds((j + 1) * GROUP, GROUP)].reshape(GROUP * BLK, HS),
                    ],
                    axis=1,
                )
                next_keys = kv_s[:, (j + 1) * HS : (j + 2) * HS]
                none = jnp.zeros((BLK, HS), jnp.bfloat16)
                both_keys = jnp.concatenate(
                    [
                        jnp.concatenate([keys, none], axis=1),
                        jnp.concatenate([none, next_keys], axis=1),
                    ],
                    axis=0,
                )
                both_scores = lax.dot_general(
                    queries, both_keys, (((1,), (1,)), ((), ())), preferred_element_type=jnp.float32
                )
            scores = both_scores[:, (j % 2) * BLK : (j % 2 + 1) * BLK]
            scores = scores.reshape(GROUP, BLK, BLK) + bias
            top = jnp.max(scores, axis=-1, keepdims=True)
            weights = jnp.exp2((scores - top) * scale).astype(jnp.bfloat16).reshape(GROUP * BLK, BLK)
            widened = jnp.concatenate([values, jnp.ones((BLK, HS), jnp.bfloat16)], axis=1)
            both = jnp.dot(weights, widened, preferred_element_type=jnp.float32)
            mixture = (both[:, :HS] / both[:, HS:]).reshape(GROUP, BLK, HS)
            states = (x_s[heads].astype(jnp.float32) + mixture).astype(jnp.bfloat16)
            if layer < 3:
                x_s[heads] = states
                squares = prepare(layer + 1, j, states, squares)
                w_copy(layer + 1, j).wait()
                if layer == 0:
                    w_copy(3, j).start()
                project(layer + 1, j)
            else:
                for g in range(GROUP):
                    cols = slice((j * GROUP + g) * HS, (j * GROUP + g + 1) * HS)
                    out_ref[:, cols] = states[g]
                    gap = states[g].astype(jnp.float32) - frozen_s[:, cols].astype(jnp.float32)
                    gaps += gap * gap
    flag = jnp.where(t < boundary, (code // 2) % 2, code % 2).astype(jnp.float32)
    part = jnp.sum(((1.0 - flag) - forget_weight * flag) * gaps, axis=0, keepdims=True)
    part = jnp.sum(part, axis=1, keepdims=True) * (1.0 / HD)
    part_ref[...] = jnp.broadcast_to(part, part_ref.shape)


def run_layers(code, pieces, gains, frozen, weights):
    vmem = pl.BlockSpec(memory_space=pltpu.VMEM)
    return pl.pallas_call(
        layers_kernel,
        out_shape=(
            jax.ShapeDtypeStruct((BLK, HD), jnp.bfloat16),
            jax.ShapeDtypeStruct((128, 1, HS), jnp.float32),
        ),
        in_specs=[
            pl.BlockSpec(memory_space=pltpu.SMEM), vmem, vmem,
            pl.BlockSpec(memory_space=pltpu.HBM),
            pl.BlockSpec(memory_space=pltpu.HBM),
        ],
        out_specs=(vmem, vmem),
        scratch_shapes=[
            pltpu.VMEM((QH, BLK, HS), jnp.bfloat16),
            pltpu.VMEM((QH, BLK, HS), jnp.bfloat16),
            pltpu.VMEM((BLK, KVW), jnp.float32),
            pltpu.VMEM((BLK, KVW), jnp.bfloat16),
            pltpu.VMEM((4, HD, KVW), jnp.bfloat16),
            pltpu.SemaphoreType.DMA((4, CHUNKS)),
            pltpu.VMEM((BLK, HD), jnp.bfloat16),
            pltpu.SemaphoreType.DMA,
        ],
        compiler_params=pltpu.CompilerParams(vmem_limit_bytes=52 << 20),
        name="layers",
    )(code, pieces, gains, frozen, weights)


def order_kernel(plan_ref, landed_ref, ordered_ref):
    def place(b, carry):
        ordered_ref[plan_ref[b]] = landed_ref[b]
        return carry

    lax.fori_loop(0, landed_ref.shape[0], place, 0, unroll=8)


def exchange(pieces):
    section_count = lax.axis_size("section")
    grid = pieces.reshape((-1, section_count) + pieces.shape[1:])
    grid = lax.all_to_all(grid, "section", split_axis=1, concat_axis=1, tiled=True)
    grid = lax.all_to_all(grid, "dp", split_axis=0, concat_axis=0, tiled=True)
    return grid.reshape(pieces.shape)


def route(hidden_in, block_plan):
    pieces = hidden_in.reshape(BLK, QH, HS).transpose(1, 0, 2).reshape(-1, PIECE_ROWS, HS)
    landed = exchange(pieces)
    vmem = pl.BlockSpec(memory_space=pltpu.VMEM)
    ordered = pl.pallas_call(
        order_kernel,
        out_shape=jax.ShapeDtypeStruct(landed.shape, landed.dtype),
        in_specs=[pl.BlockSpec(memory_space=pltpu.SMEM), vmem],
        out_specs=vmem,
        name="order",
    )(block_plan, landed)
    arrived = exchange(ordered)
    return arrived.reshape(QH, BLK, HS)


def local(hidden_in, segments, forget_flags, block_plan, layer_gains, kv_weights, frozen_states):
    device_count = lax.axis_size("dp") * lax.axis_size("section")
    here = lax.axis_index(ALL)
    weights = lax.all_gather(kv_weights[0], ("section", "dp"), axis=0, tiled=True)
    weights = weights.reshape(4, HD, KVW)
    boundary = BLK - jnp.sum(segments[0])
    pieces = route(hidden_in, block_plan)
    sample = pieces[0, 0, 0]
    later = (sample != sample).astype(jnp.int32)
    code = jnp.concatenate([(boundary + later).reshape(1), forget_flags[0]]).astype(jnp.bfloat16)
    code = jnp.zeros((1, HS), jnp.bfloat16).at[0, :3].set(code)
    own_gains = lax.dynamic_slice(layer_gains, (0, lax.axis_index("dp") * HS), (1, HS))
    message = jnp.concatenate([own_gains, code], axis=0)
    messages = lax.all_to_all(
        jnp.broadcast_to(message[None], (device_count, 2, HS)), ALL, split_axis=0, concat_axis=0, tiled=True
    )
    gains = messages[:, 0].reshape(QH, 4, HS).transpose(1, 0, 2).reshape(4, QH, 1, HS)
    codes = messages[:, 1].astype(jnp.float32)
    routed = jnp.sum(jnp.where((block_plan == here)[:, None], codes, 0.0), axis=0)
    routed_code = (routed[0] * 4.0 + routed[1] * 2.0 + routed[2]).astype(jnp.int32).reshape(1)
    finished, part = run_layers(routed_code, pieces, gains, frozen_states, weights)
    parts = lax.all_to_all(part, ALL, split_axis=0, concat_axis=0, tiled=True)
    objective = jnp.sum(parts[:, 0, 0]) / (BLK * device_count)
    return finished, objective


def solution(mesh):
    in_specs = (
        P(ALL, None),
        P(ALL, None),
        P(ALL, None),
        P(),
        P("section", None),
        P("section", "dp", None),
        P(ALL, None),
    )
    out_specs = (P(ALL, None), P())
    return jax.shard_map(local, mesh=mesh, in_specs=in_specs, out_specs=out_specs, check_vma=False)
```

```python
import math

import jax
import jax.numpy as jnp
from jax import lax
from jax.experimental import pallas as pl
from jax.experimental.pallas import tpu as pltpu
from jax.sharding import PartitionSpec as P

QH = 32
KVH = 4
HS = 128
GROUP = 8
BLK = 128
HD = 4096
KVW = 2 * KVH * HS
PIECE_ROWS = 32
CHUNKS = 4

forget_weight = 0.5
ALL = ("dp", "section")


def layers_kernel(
    code_ref, pieces_ref, gain_ref, frozen_ref, w_ref, out_ref, part_ref,
    x_s, scaled_s, acc_s, kv_s, w_buf, sems, frozen_s, frozen_sem,
):
    depth = HD // CHUNKS

    def w_copy(layer, c):
        slabs = pl.ds(c * GROUP, GROUP)
        return pltpu.make_async_copy(
            w_ref.at[slabs, layer], w_buf.at[layer, slabs], sems.at[layer, c]
        )

    def prepare(layer, j, states, squares):
        heads = pl.ds(j * GROUP, GROUP)
        widened = states.astype(jnp.float32)
        gain = gain_ref[layer, heads].astype(jnp.float32)
        scaled_s[heads] = (widened * gain).astype(jnp.bfloat16)
        return squares + jnp.sum(widened * widened, axis=0)

    def project(layer, j):
        rows = jnp.concatenate([scaled_s[j * GROUP + i] for i in range(GROUP)], axis=1)
        part = jnp.dot(
            rows, w_buf[layer, j * GROUP : (j + 1) * GROUP].reshape(depth, KVW), preferred_element_type=jnp.float32
        )
        if j == 0:
            acc_s[...] = part
        else:
            acc_s[...] += part

    for layer in range(2):
        for c in range(CHUNKS):
            w_copy(layer, c).start()
    frozen_copy = pltpu.make_async_copy(frozen_ref, frozen_s, frozen_sem)
    frozen_copy.start()
    code = code_ref[0]
    boundary = code // 4
    t = lax.broadcasted_iota(jnp.int32, (BLK, BLK), 0)
    s = lax.broadcasted_iota(jnp.int32, (BLK, BLK), 1)
    allowed = (s <= t) & ((t < boundary) == (s < boundary))
    bias = jnp.where(allowed, 0.0, -jnp.inf)[None]
    factor = math.log2(math.e) / math.sqrt(HS)
    squares = jnp.zeros((BLK, HS), jnp.float32)
    for j in range(KVH):
        heads = pl.ds(j * GROUP, GROUP)
        states = pieces_ref[heads]
        x_s[heads] = states
        squares = prepare(0, j, states, squares)
    for j in range(KVH):
        w_copy(0, j).wait()
        w_copy(2, j).start()
        project(0, j)
    gaps = jnp.zeros((BLK, HS), jnp.float32)
    for layer in range(4):
        inverse = lax.rsqrt(jnp.sum(squares, axis=-1, keepdims=True) * (1.0 / HD) + 1e-05)
        kv_s[...] = (acc_s[...] * inverse).astype(jnp.bfloat16)
        scale = (inverse * factor)[None]
        squares = jnp.zeros((BLK, HS), jnp.float32)
        if layer == 3:
            frozen_copy.wait()
        for j in range(KVH):
            keys = kv_s[:, j * HS : (j + 1) * HS]
            values = kv_s[:, (j + KVH) * HS : (j + KVH + 1) * HS]
            heads = pl.ds(j * GROUP, GROUP)
            if j % 2 == 0:
                queries = jnp.concatenate(
                    [
                        scaled_s[heads].reshape(GROUP * BLK, HS),
                        scaled_s[pl.ds((j + 1) * GROUP, GROUP)].reshape(GROUP * BLK, HS),
                    ],
                    axis=1,
                )
                next_keys = kv_s[:, (j + 1) * HS : (j + 2) * HS]
                none = jnp.zeros((BLK, HS), jnp.bfloat16)
                both_keys = jnp.concatenate(
                    [
                        jnp.concatenate([keys, none], axis=1),
                        jnp.concatenate([none, next_keys], axis=1),
                    ],
                    axis=0,
                )
                both_scores = lax.dot_general(
                    queries, both_keys, (((1,), (1,)), ((), ())), preferred_element_type=jnp.float32
                )
            scores = both_scores[:, (j % 2) * BLK : (j % 2 + 1) * BLK]
            scores = scores.reshape(GROUP, BLK, BLK) + bias
            top = jnp.max(scores, axis=-1, keepdims=True)
            weights = jnp.exp2((scores - top) * scale).astype(jnp.bfloat16).reshape(GROUP * BLK, BLK)
            widened = jnp.concatenate([values, jnp.ones((BLK, HS), jnp.bfloat16)], axis=1)
            both = jnp.dot(weights, widened, preferred_element_type=jnp.float32)
            mixture = (both[:, :HS] / both[:, HS:]).reshape(GROUP, BLK, HS)
            states = (x_s[heads].astype(jnp.float32) + mixture).astype(jnp.bfloat16)
            if layer < 3:
                x_s[heads] = states
                squares = prepare(layer + 1, j, states, squares)
                w_copy(layer + 1, j).wait()
                if layer == 0:
                    w_copy(3, j).start()
                project(layer + 1, j)
            else:
                for g in range(GROUP):
                    cols = slice((j * GROUP + g) * HS, (j * GROUP + g + 1) * HS)
                    out_ref[:, cols] = states[g]
                    gap = states[g].astype(jnp.float32) - frozen_s[:, cols].astype(jnp.float32)
                    gaps += gap * gap
    flag = jnp.where(t < boundary, (code // 2) % 2, code % 2).astype(jnp.float32)
    part = jnp.sum(((1.0 - flag) - forget_weight * flag) * gaps, axis=0, keepdims=True)
    part = jnp.sum(part, axis=1, keepdims=True) * (1.0 / HD)
    part_ref[...] = jnp.broadcast_to(part, part_ref.shape)


def run_layers(code, pieces, gains, frozen, weights):
    vmem = pl.BlockSpec(memory_space=pltpu.VMEM)
    return pl.pallas_call(
        layers_kernel,
        out_shape=(
            jax.ShapeDtypeStruct((BLK, HD), jnp.bfloat16),
            jax.ShapeDtypeStruct((128, 1, HS), jnp.float32),
        ),
        in_specs=[
            pl.BlockSpec(memory_space=pltpu.SMEM), vmem, vmem,
            pl.BlockSpec(memory_space=pltpu.HBM),
            pl.BlockSpec(memory_space=pltpu.HBM),
        ],
        out_specs=(vmem, vmem),
        scratch_shapes=[
            pltpu.VMEM((QH, BLK, HS), jnp.bfloat16),
            pltpu.VMEM((QH, BLK, HS), jnp.bfloat16),
            pltpu.VMEM((BLK, KVW), jnp.float32),
            pltpu.VMEM((BLK, KVW), jnp.bfloat16),
            pltpu.VMEM((4, QH, HS, KVW), jnp.bfloat16),
            pltpu.SemaphoreType.DMA((4, CHUNKS)),
            pltpu.VMEM((BLK, HD), jnp.bfloat16),
            pltpu.SemaphoreType.DMA,
        ],
        compiler_params=pltpu.CompilerParams(vmem_limit_bytes=52 << 20),
        name="layers",
    )(code, pieces, gains, frozen, weights)


def order_kernel(plan_ref, landed_ref, ordered_ref):
    def place(b, carry):
        ordered_ref[plan_ref[b]] = landed_ref[b]
        return carry

    lax.fori_loop(0, landed_ref.shape[0], place, 0, unroll=8)


def route(hidden_in, block_plan):
    pieces = hidden_in.reshape(BLK, QH, HS).transpose(1, 0, 2).reshape(-1, PIECE_ROWS, HS)
    landed = lax.all_to_all(pieces, ALL, split_axis=0, concat_axis=0, tiled=True)
    vmem = pl.BlockSpec(memory_space=pltpu.VMEM)
    ordered = pl.pallas_call(
        order_kernel,
        out_shape=jax.ShapeDtypeStruct(landed.shape, landed.dtype),
        in_specs=[pl.BlockSpec(memory_space=pltpu.SMEM), vmem],
        out_specs=vmem,
        name="order",
    )(block_plan, landed)
    arrived = lax.all_to_all(ordered, ALL, split_axis=0, concat_axis=0, tiled=True)
    return arrived.reshape(QH, BLK, HS)


def local(hidden_in, segments, forget_flags, block_plan, layer_gains, kv_weights, frozen_states):
    device_count = lax.axis_size("dp") * lax.axis_size("section")
    here = lax.axis_index(ALL)
    weights = lax.all_gather(kv_weights[0], ALL, axis=0, tiled=True)
    weights = weights.reshape(QH, 4, HS, KVW)
    boundary = BLK - jnp.sum(segments[0])
    pieces = route(hidden_in, block_plan)
    sample = pieces[0, 0, 0]
    later = (sample != sample).astype(jnp.int32)
    code = jnp.concatenate([(boundary + later).reshape(1), forget_flags[0]]).astype(jnp.bfloat16)
    code = jnp.zeros((1, HS), jnp.bfloat16).at[0, :3].set(code)
    own_gains = lax.dynamic_slice(layer_gains, (0, lax.axis_index("dp") * HS), (1, HS))
    message = jnp.concatenate([own_gains, code], axis=0)
    messages = lax.all_to_all(
        jnp.broadcast_to(message[None], (device_count, 2, HS)), ALL, split_axis=0, concat_axis=0, tiled=True
    )
    gains = messages[:, 0].reshape(QH, 4, HS).transpose(1, 0, 2).reshape(4, QH, 1, HS)
    codes = messages[:, 1].astype(jnp.float32)
    routed = jnp.sum(jnp.where((block_plan == here)[:, None], codes, 0.0), axis=0)
    routed_code = (routed[0] * 4.0 + routed[1] * 2.0 + routed[2]).astype(jnp.int32).reshape(1)
    finished, part = run_layers(routed_code, pieces, gains, frozen_states, weights)
    parts = lax.all_to_all(part, ALL, split_axis=0, concat_axis=0, tiled=True)
    objective = jnp.sum(parts[:, 0, 0]) / (BLK * device_count)
    return finished, objective


def solution(mesh):
    in_specs = (
        P(ALL, None),
        P(ALL, None),
        P(ALL, None),
        P(),
        P("section", None),
        P("section", "dp", None),
        P(ALL, None),
    )
    out_specs = (P(ALL, None), P())
    return jax.shard_map(local, mesh=mesh, in_specs=in_specs, out_specs=out_specs, check_vma=False)
```
